32 devices in a mesh: blk: 2 (over y), uly: 4 (over z), tp: 4 (over x, core).
Axes of the slice: x: 2, y: 2, z: 4, core: 2. Of those that a mesh axis runs over, the one named last changes fastest.
Arguments:
- queries: bfloat16 [1024, 8192], P(('blk', 'uly'), 'tp'), parts along dimension 1, may hold values from -9 to 9
- keys: bfloat16 [1024, 1024], P(('blk', 'uly'), 'tp'), parts along dimension 1, may hold values from -9 to 9
- values: bfloat16 [1024, 1024], P(('blk', 'uly'), 'tp'), parts along dimension 1, may hold values from -6 to 6
- head_map: int32 [64], P('tp'), parts along dimension 0, may hold values from 0 to 1, as said below
- doc_lengths: int32 [8], replicated, may hold values from 1 to 512, 1024 in all
- plan: int32 [2, 8], replicated, may hold values from 0 to 7, as said below
Outputs:
- output: bfloat16 [1024, 8192], P(('blk', 'uly'), 'tp'), parts along dimension 1
The draws below stay inside these ranges and needn't reach their ends.
There are 4 independent parts, one for each index of `tp`. The reference program is written for one: setup_inputs(seed, part) draws one part's arguments, and reference() takes and returns one part's arrays. A program takes and returns all parts, laid end to end along the dimension named above; an argument that names none is the same for every part. Nothing has to cross between parts.
Inputs may be any that keep to these rules, and one draw needn't show every extreme that they name: `head_map`: each key-value head serves exactly 8 query heads. Each row plan[s] is a permutation of 0 to 7.
All inputs are finite; a program needn't handle non-finite values.
Results may differ from the reference program's by a relative error of at most 0.0036.
Values may be sent and summed in bfloat16 or wider, within the bound.
No kernel may reach another device: no remote copies, remote signals or barrier semaphores. Data moves between devices by JAX's collectives and lax.ppermute only.
A program may use at most 64 MiB of HBM per device.

```python
import math
import jax
import jax.numpy as jnp
import numpy as np
from jax import lax

DH = 128
HEADS = 16
KVH = 2
STRETCHES = 2
SEQ = 1024
PIECES = 8
BLOCK = 64
MOSTDOC = 512
NDOCS = 8


def draw_queries(key, part):
    base_key = jax.random.fold_in(key, 1)
    base = jax.random.truncated_normal(base_key, -4.0, 4.0, (SEQ, HEADS * DH), jnp.float32)
    return base.astype(jnp.bfloat16)


def draw_keys(key, part):
    base_key = jax.random.fold_in(key, 2)
    base = jax.random.truncated_normal(base_key, -4.0, 4.0, (SEQ, KVH * DH), jnp.float32)
    return base.astype(jnp.bfloat16)


def draw_head_map(key, part):
    order = jax.random.permutation(jax.random.fold_in(key, 3), HEADS)
    return (order % KVH).astype(jnp.int32)


def draw_plan(key, part):
    row_keys = jax.random.split(jax.random.fold_in(key, 5), STRETCHES)
    rows = jax.vmap(lambda row_key: jax.random.permutation(row_key, PIECES))(row_keys)
    return rows.astype(jnp.int32)


def shard_levels(own_key, dims, cuts, low, high):
    level, own = 1.0, jax.random.fold_in(own_key, 6)
    for axis_at, shards_of in cuts:
        steps = jnp.exp(jax.random.uniform(jax.random.fold_in(own, axis_at), (shards_of,), jnp.float32, low / len(cuts), high / len(cuts)))
        level = level * jnp.repeat(steps, dims[axis_at] // shards_of).reshape([-1 if axis == axis_at else 1 for axis in range(len(dims))])
    return level


def length_profile(count, total, reach, skew):
    portions = [(1 << 20) // math.isqrt(rank ** skew) + 1 for rank in range(2, count + 1)]
    surplus, given = total - reach - (count - 1), [1] * (count - 1)
    while surplus > 0:
        movable = [i for i in range(count - 1) if given[i] < reach]
        mass, left = sum([portions[i] for i in movable]), surplus
        for i in movable:
            extra = min(reach - given[i], max(1, left * portions[i] // mass), surplus)
            given[i] = given[i] + extra
            surplus = surplus - extra
    return np.array([reach] + given)


def uneven(key, amount, total, limit, lean):
    if amount == 2:
        one = jax.random.randint(key, (), max(1, total - limit), min(limit, total - 1) + 1)
        return jnp.stack([one, total - one])
    tallies = jnp.asarray(length_profile(amount, total, limit, lean), jnp.int32)
    twos = (amount - 1) // 2
    source_of, sink = tallies[1:1 + 2 * twos:2], tallies[2:2 + 2 * twos:2]
    room = jnp.minimum(source_of - 1, limit - sink)
    moved = jax.random.randint(jax.random.fold_in(key, 1), (twos,), 0, 1 << 20) % (room + 1)
    tallies = tallies.at[1:1 + 2 * twos:2].set(source_of - moved).at[2:2 + 2 * twos:2].set(sink + moved)
    return tallies[jax.random.permutation(jax.random.fold_in(key, 2), amount)]


def bell_draw(key, extent, spread, reach, cuts=(), kind=jnp.bfloat16):
    values = jax.random.normal(key, extent, jnp.float32) * spread
    if len(cuts) > 0:
        values = shard_levels(key, extent, cuts, -0.22, 0.18) * values
    return jnp.clip(values, min=-reach, max=reach).astype(kind)


def setup_inputs(seed: int = 0, part: int = 0) -> dict:
    splits = jax.random.split(jax.random.key(seed), 7)
    own_keys = jax.random.split(jax.random.fold_in(splits[6], part), 7)
    queries = draw_queries(jax.random.fold_in(jax.random.fold_in(splits[6], part), 71), part)
    keys = draw_keys(jax.random.fold_in(jax.random.fold_in(splits[6], part), 71), part)
    values = bell_draw(own_keys[2], (SEQ, KVH * DH), 1.0, 6.0, ((0, 8),))
    head_map = draw_head_map(jax.random.fold_in(jax.random.fold_in(splits[6], part), 71), part)
    doc_lengths = uneven(splits[4], NDOCS, SEQ, MOSTDOC, 2).astype(jnp.int32)
    plan = draw_plan(jax.random.fold_in(splits[6], 71), part)
    return dict(queries=queries, keys=keys, values=values, head_map=head_map, doc_lengths=doc_lengths, plan=plan)


def reference(queries, keys, values, head_map, doc_lengths, plan):
    seq_rows = queries.shape[0]
    query_rows = queries.reshape(seq_rows, HEADS, DH)
    key_rows = keys.reshape(seq_rows, KVH, DH)[:, head_map]
    value_rows = values.reshape(seq_rows, KVH, DH)[:, head_map]
    doc_ends = jnp.cumsum(doc_lengths).astype(jnp.int32)
    positions = jnp.arange(seq_rows, dtype=jnp.int32)
    doc_of = lax.optimization_barrier(jnp.sum((positions[:, None] >= doc_ends[None, :]).astype(jnp.int32), axis=1)).astype(jnp.int32)
    tile = math.gcd(256, seq_rows)
    span = MOSTDOC + tile
    key_padded = jnp.pad(key_rows, ((MOSTDOC, 0), (0, 0), (0, 0)))
    value_padded = jnp.pad(value_rows, ((MOSTDOC, 0), (0, 0), (0, 0)))
    doc_padded = jnp.concatenate([jnp.full((MOSTDOC,), -1, jnp.int32), doc_of])
    scale = 1.0 / math.sqrt(DH)

    def one_tile(tile_index):
        first = (tile_index * tile).astype(jnp.int32)
        query_tile = lax.dynamic_slice_in_dim(query_rows, first, tile, 0).astype(jnp.float32)
        key_tile = lax.dynamic_slice_in_dim(key_padded, first, span, 0).astype(jnp.float32)
        value_tile = lax.dynamic_slice_in_dim(value_padded, first, span, 0).astype(jnp.float32)
        query_doc = lax.dynamic_slice_in_dim(doc_of, first, tile, 0)
        key_doc = lax.dynamic_slice_in_dim(doc_padded, first, span, 0)
        query_pos = first + jnp.arange(tile, dtype=jnp.int32)
        key_pos = first - MOSTDOC + jnp.arange(span, dtype=jnp.int32)
        visible = (query_doc[:, None] == key_doc[None, :]) & (key_pos[None, :] <= query_pos[:, None])
        scores = jnp.einsum('thd,shd->ths', query_tile, key_tile) * scale
        scores = jnp.where(visible[:, None, :], scores, -jnp.inf)
        top = lax.optimization_barrier(jnp.max(scores, axis=-1))
        expo = jnp.exp(scores - top[..., None])
        total = lax.optimization_barrier(jnp.sum(expo, axis=-1))
        weights = lax.optimization_barrier(expo.astype(jnp.bfloat16)).astype(jnp.float32)
        summed = jnp.einsum('ths,shd->thd', weights, value_tile)
        return (summed / total[..., None]).astype(jnp.bfloat16)
    attended = lax.map(one_tile, jnp.arange(seq_rows // tile, dtype=jnp.int32))
    attended = attended.reshape(STRETCHES, PIECES, BLOCK, HEADS * DH)
    picked = attended[jnp.arange(STRETCHES, dtype=jnp.int32)[:, None], plan]
    picked = picked.reshape(STRETCHES, STRETCHES, PIECES // STRETCHES, BLOCK, HEADS * DH)
    return jnp.swapaxes(picked, 0, 1).reshape(seq_rows, HEADS * DH)
```

```python
import functools
import math

import jax
import jax.numpy as jnp
from jax import lax
from jax.experimental import pallas as pl
from jax.experimental.pallas import tpu as pltpu
from jax.sharding import PartitionSpec as P

DH = 128
LOG2E = 1.4426950408889634


VMEM = pl.BlockSpec(memory_space=pltpu.VMEM)
SMEM = pl.BlockSpec(memory_space=pltpu.SMEM)


def sort_heads(map_ref, order_ref, count_ref, kv_heads):
    heads = map_ref.shape[0]
    per = heads // kv_heads
    for kv in range(kv_heads):
        count_ref[kv] = 0
    for h in range(heads):
        kv = map_ref[h]
        n = count_ref[kv]
        order_ref[kv * per + n] = h
        count_ref[kv] = n + 1


def pack_kernel(geo, map_ref, q_ref, k_ref, v_ref, *rest):
    B, C, lh, kv_heads = geo["B"], geo["C"], geo["lh"], geo["kv_heads"]
    outs, (order_ref, count_ref) = rest[:-2], rest[-2:]
    y, z = lax.axis_index("blk"), lax.axis_index("uly")
    for d in range(C):
        kv_out = outs[B * C + d]
        col = pl.multiple_of(lax.rem(z + d, C) * kv_heads // C * DH, DH)
        kv_out[0] = k_ref[:, pl.ds(col, DH)]
        kv_out[1] = v_ref[:, pl.ds(col, DH)]
    sort_heads(map_ref, order_ref, count_ref, kv_heads)
    for m in range(B):
        for d in range(C):
            group = lax.rem(z + d, C) * B + lax.rem(y + m, B)
            for i in range(lh):
                h = order_ref[group * lh + i]
                outs[m * C + d][i] = q_ref[:, pl.ds(pl.multiple_of(h * DH, DH), DH)]


def gather_kv_kernel(geo, *refs):
    U = geo["U"]
    z = lax.axis_index("uly")
    out = refs[-1]
    for k in range(U):
        source = lax.rem(z - k + U, U)
        out[0, source] = refs[k][0]
        out[1, source] = refs[k][1]


def attend_kernel(geo, lengths_ref, plan_ref, *refs):
    B, C, U, lh = geo["B"], geo["C"], geo["U"], geo["lh"]
    block, pieces, tokens = geo["block"], geo["pieces"], geo["tokens"]
    stretch = tokens * U
    kv_refs, refs = refs[:B], refs[B:]
    own_q, refs = refs[:U], refs[U:]
    far_q, refs = refs[:U], refs[U:]
    outs, (kv_cat, q_cat) = refs[:-2], refs[-2:]
    y, z = lax.axis_index("blk"), lax.axis_index("uly")
    s, c = z // C, lax.rem(z, C)

    @pl.when(s == 0)
    def _():
        kv_cat[:, :U] = jnp.zeros((2, U, tokens, DH), kv_cat.dtype)

    for m in range(B):
        holder = lax.rem(y - m + B, B)

        @pl.when(holder == s)
        def _():
            kv_cat[:, U:] = kv_refs[m][...]

        @pl.when(holder == s - 1)
        def _():
            kv_cat[:, :U] = kv_refs[m][...]

    for k in range(U):
        source = lax.rem(z - k + U, U)

        @pl.when(y == s)
        def _():
            q_cat[source] = own_q[k][...]

        @pl.when(y != s)
        def _():
            q_cat[source] = far_q[k][...]

    ends = []
    total = 0
    for n in range(lengths_ref.shape[0]):
        total = total + lengths_ref[n]
        ends.append(total)
    per_tile = tokens // block
    span = stretch + tokens
    slots = pieces // (B * C)
    factor = LOG2E / math.sqrt(DH)
    for db in range(B):
        for dc in range(C):
            out = outs[db * C + dc]
            first = lax.rem(y + db, B) * (pieces // B) + lax.rem(c + dc, C) * slots
            for j in range(slots):
                p = plan_ref[s, first + j]
                tile = p // per_tile
                inside = pl.multiple_of((p - tile * per_tile) * block, block)
                q = q_cat[tile, :, pl.ds(inside, block), :].reshape(lh * block, DH)
                k = kv_cat[0, pl.ds(tile, U + 1)].reshape(span, DH)
                v = kv_cat[1, pl.ds(tile, U + 1)].reshape(span, DH)
                score = lax.dot_general(
                    q, k, (((1,), (1,)), ((), ())), preferred_element_type=jnp.float32
                )
                row = lax.broadcasted_iota(jnp.int32, (block, 1), 0)
                at = row + (s * stretch + p * block)
                start = jnp.zeros((block, 1), jnp.int32)
                for end in ends:
                    start = jnp.maximum(start, jnp.where(at >= end, end, 0))
                base = (s - 1) * stretch + tile * tokens
                key = lax.broadcasted_iota(jnp.int32, (block, span), 1)
                seen = (key >= start - base) & (key <= at - base)
                score = jnp.where(seen[None], score.reshape(lh, block, span), -jnp.inf)
                top = jnp.max(score, axis=-1, keepdims=True)
                expo = jnp.exp2((score - top) * factor)
                norm = jnp.sum(expo, axis=-1, keepdims=True)
                summed = jnp.dot(
                    expo.astype(jnp.bfloat16).reshape(lh * block, span),
                    v,
                    preferred_element_type=jnp.float32,
                )
                result = summed.reshape(lh, block, DH) / norm
                out[:, j * block : (j + 1) * block, :] = result.astype(jnp.bfloat16)


def unpack_kernel(geo, map_ref, *rest):
    B, C, lh, kv_heads = geo["B"], geo["C"], geo["lh"], geo["kv_heads"]
    pieces, (out, order_ref, count_ref) = rest[:-3], rest[-3:]
    y, z = lax.axis_index("blk"), lax.axis_index("uly")
    sort_heads(map_ref, order_ref, count_ref, kv_heads)
    for db in range(B):
        for dc in range(C):
            group = lax.rem(z - dc + C, C) * B + lax.rem(y - db + B, B)
            for i in range(lh):
                h = order_ref[group * lh + i]
                out[:, pl.ds(pl.multiple_of(h * DH, DH), DH)] = pieces[db * C + dc][i]


def body(queries, keys, values, head_map, doc_lengths, plan):
    B, U = lax.axis_size("blk"), lax.axis_size("uly")
    C = U // B
    tokens, heads = queries.shape[0], head_map.shape[0]
    kv_heads = keys.shape[1] // DH
    lh = heads // U
    pieces = plan.shape[1]
    stretch = tokens * U
    block = stretch // pieces
    assert B * C == U and C % kv_heads == 0 and tokens % block == 0
    geo = dict(
        B=B, U=U, C=C, lh=lh, kv_heads=kv_heads, block=block, pieces=pieces, tokens=tokens
    )
    bf16 = jnp.bfloat16
    group_shape = jax.ShapeDtypeStruct((lh, tokens, DH), bf16)
    piece_shape = jax.ShapeDtypeStruct((2, tokens, DH), bf16)
    sort_scratch = [pltpu.SMEM((heads,), jnp.int32), pltpu.SMEM((kv_heads,), jnp.int32)]
    axes = ("blk", "uly")
    y, z = lax.axis_index("blk"), lax.axis_index("uly")

    def permute(x, target, wanted=lambda y, z: True):
        pairs = [
            (a * U + b, target(a, b)[0] * U + target(a, b)[1])
            for a in range(B)
            for b in range(U)
            if wanted(a, b)
        ]
        return lax.ppermute(x, axes, pairs)

    packed = pl.pallas_call(
        functools.partial(pack_kernel, geo),
        out_shape=[group_shape] * (B * C) + [piece_shape] * C,
        in_specs=[SMEM, VMEM, VMEM, VMEM],
        out_specs=[VMEM] * (B * C + C),
        scratch_shapes=sort_scratch,
        name="pack",
    )(head_map, queries, keys, values)
    groups = [packed[m * C : (m + 1) * C] for m in range(B)]
    own, kv_parts = groups[0], packed[B * C :]

    kv_in = [kv_parts[0]]
    for k in range(1, U):
        kv_in.append(
            permute(
                kv_parts[k % C],
                lambda a, b, k=k: (a, (b + k) % U),
                lambda a, b, k=k: (b + k) % U // C in (a, a + 1),
            )
        )
    crossed = [
        [permute(x, lambda a, b, m=m: ((a + m) % B, b)) for x in groups[m]] for m in range(1, B)
    ]
    own_q = [own[0]]
    for k in range(1, U):
        own_q.append(
            permute(
                own[k % C],
                lambda a, b, k=k: (a, (b + k) % U),
                lambda a, b, k=k: (b + k) % U // C == a,
            )
        )
    kv_own = pl.pallas_call(
        functools.partial(gather_kv_kernel, geo),
        out_shape=jax.ShapeDtypeStruct((2, U, tokens, DH), bf16),
        in_specs=[VMEM] * U,
        out_specs=VMEM,
        name="gather_kv",
    )(*kv_in)
    kv_all = [kv_own]
    for m in range(1, B):
        kv_all.append(
            permute(
                kv_own,
                lambda a, b, m=m: ((a + m) % B, b),
                lambda a, b: b // C in (a, a + 1),
            )
        )
    far_q = []
    for k in range(U):
        if B == 2:
            x = crossed[0][k % C]
        else:
            step = (y - (z + k) % U // C) % B
            x = lax.dynamic_index_in_dim(
                jnp.stack([rows[k % C] for rows in crossed]), jnp.maximum(step - 1, 0), 0, False
            )
        if k:
            x = permute(
                x,
                lambda a, b, k=k: (a, (b + k) % U),
                lambda a, b, k=k: (b + k) % U // C != a,
            )
        far_q.append(x)

    sent = pl.pallas_call(
        functools.partial(attend_kernel, geo),
        out_shape=[group_shape] * (B * C),
        in_specs=[SMEM, SMEM] + [VMEM] * (B + 2 * U),
        out_specs=[VMEM] * (B * C),
        scratch_shapes=[
            pltpu.VMEM((2, 2 * U, tokens, DH), bf16),
            pltpu.VMEM((U, lh, tokens, DH), bf16),
        ],
        compiler_params=pltpu.CompilerParams(vmem_limit_bytes=48 * 1024 * 1024),
        name="attend",
    )(doc_lengths, plan, *kv_all, *own_q, *far_q)

    arrived = [
        permute(
            sent[db * C + dc],
            lambda a, b, db=db, dc=dc: ((a + db) % B, b // C * C + (b + dc) % C),
        )
        if db or dc
        else sent[0]
        for db in range(B)
        for dc in range(C)
    ]
    return pl.pallas_call(
        functools.partial(unpack_kernel, geo),
        out_shape=jax.ShapeDtypeStruct((tokens, heads * DH), bf16),
        in_specs=[SMEM] + [VMEM] * (B * C),
        out_specs=VMEM,
        scratch_shapes=sort_scratch,
        name="unpack",
    )(head_map, *arrived)


def solution(mesh):
    return jax.shard_map(
        body,
        mesh=mesh,
        in_specs=(
            P(("blk", "uly"), "tp"),
            P(("blk", "uly"), "tp"),
            P(("blk", "uly"), "tp"),
            P("tp"),
            P(),
            P(),
        ),
        out_specs=P(("blk", "uly"), "tp"),
        check_vma=False,
    )
```

```python
import functools
import math

import jax
import jax.numpy as jnp
from jax import lax
from jax.experimental import pallas as pl
from jax.experimental.pallas import tpu as pltpu
from jax.sharding import PartitionSpec as P

DH = 128
LOG2E = 1.4426950408889634


VMEM = pl.BlockSpec(memory_space=pltpu.VMEM)
SMEM = pl.BlockSpec(memory_space=pltpu.SMEM)


def sort_heads(map_ref, order_ref, count_ref, kv_heads):
    heads = map_ref.shape[0]
    per = heads // kv_heads
    for kv in range(kv_heads):
        count_ref[kv] = 0
    for h in range(heads):
        kv = map_ref[h]
        n = count_ref[kv]
        order_ref[kv * per + n] = h
        count_ref[kv] = n + 1


def pack_kv_kernel(geo, k_ref, v_ref, *outs):
    C, kv_heads = geo["C"], geo["kv_heads"]
    z = lax.axis_index("uly")
    for d in range(C):
        col = pl.multiple_of(lax.rem(z + d, C) * kv_heads // C * DH, DH)
        outs[d][0] = k_ref[:, pl.ds(col, DH)]
        outs[d][1] = v_ref[:, pl.ds(col, DH)]


def pack_kernel(geo, map_ref, q_ref, *rest):
    B, C, lh = geo["B"], geo["C"], geo["lh"]
    outs, (order_ref, count_ref) = rest[:-2], rest[-2:]
    y, z = lax.axis_index("blk"), lax.axis_index("uly")
    sort_heads(map_ref, order_ref, count_ref, geo["kv_heads"])
    for m in range(B):
        for d in range(C):
            group = lax.rem(z + d, C) * B + lax.rem(y + m, B)
            for i in range(lh):
                h = order_ref[group * lh + i]
                outs[m * C + d][i] = q_ref[:, pl.ds(pl.multiple_of(h * DH, DH), DH)]


def gather_kv_kernel(geo, *refs):
    B, C = geo["B"], geo["C"]
    z = lax.axis_index("uly")
    out = refs[-1]
    for j in range(B):
        for d in range(C):
            source = lax.rem(z // C - j + B, B) * C + lax.rem(lax.rem(z, C) - d + C, C)
            out[0, source] = refs[j * C + d][0]
            out[1, source] = refs[j * C + d][1]


def attend_kernel(geo, lengths_ref, plan_ref, *refs):
    B, C, U, lh = geo["B"], geo["C"], geo["U"], geo["lh"]
    block, pieces, tokens = geo["block"], geo["pieces"], geo["tokens"]
    stretch = tokens * U
    kv_refs, refs = refs[:B], refs[B:]
    same, refs = refs[:C], refs[C:]
    crossed, refs = refs[: (B - 1) * C], refs[(B - 1) * C :]
    across, refs = refs[: (B - 1) * C], refs[(B - 1) * C :]
    outs, (kv_cat, q_cat) = refs[:-2], refs[-2:]
    y, z = lax.axis_index("blk"), lax.axis_index("uly")
    s, c = z // C, lax.rem(z, C)

    @pl.when(s == 0)
    def _():
        kv_cat[:, :U] = jnp.zeros((2, U, tokens, DH), kv_cat.dtype)

    for m in range(B):
        holder = lax.rem(y - m + B, B)

        @pl.when(holder == s)
        def _():
            kv_cat[:, U:] = kv_refs[m][...]

        @pl.when(holder == s - 1)
        def _():
            kv_cat[:, :U] = kv_refs[m][...]

    for d in range(C):
        side = lax.rem(c - d + C, C)
        for j in range(1, B):
            q_cat[lax.rem(s - j + B, B) * C + side] = across[(j - 1) * C + d][...]
        for m in range(B):

            @pl.when(lax.rem(y - s + B, B) == m)
            def _():
                q_cat[s * C + side] = (same[d] if m == 0 else crossed[(m - 1) * C + d])[...]

    ends = []
    total = 0
    for n in range(lengths_ref.shape[0]):
        total = total + lengths_ref[n]
        ends.append(total)
    per_tile = tokens // block
    span = stretch + tokens
    slots = pieces // (B * C)
    factor = LOG2E / math.sqrt(DH)
    for db in range(B):
        for dc in range(C):
            out = outs[db * C + dc]
            first = lax.rem(y + db, B) * (pieces // B) + lax.rem(c + dc, C) * slots
            for j in range(slots):
                p = plan_ref[s, first + j]
                tile = p // per_tile
                inside = pl.multiple_of((p - tile * per_tile) * block, block)
                q = q_cat[tile, :, pl.ds(inside, block), :].reshape(lh * block, DH)
                k = kv_cat[0, pl.ds(tile, U + 1)].reshape(span, DH)
                v = kv_cat[1, pl.ds(tile, U + 1)].reshape(span, DH)
                score = lax.dot_general(
                    q, k, (((1,), (1,)), ((), ())), preferred_element_type=jnp.float32
                )
                row = lax.broadcasted_iota(jnp.int32, (block, 1), 0)
                at = row + (s * stretch + p * block)
                start = jnp.zeros((block, 1), jnp.int32)
                for end in ends:
                    start = jnp.maximum(start, jnp.where(at >= end, end, 0))
                base = (s - 1) * stretch + tile * tokens
                key = lax.broadcasted_iota(jnp.int32, (block, span), 1)
                seen = (key >= start - base) & (key <= at - base)
                score = jnp.where(seen[None], score.reshape(lh, block, span), -jnp.inf)
                top = jnp.max(score, axis=-1, keepdims=True)
                expo = jnp.exp2((score - top) * factor)
                norm = jnp.sum(expo, axis=-1, keepdims=True)
                summed = jnp.dot(
                    expo.astype(jnp.bfloat16).reshape(lh * block, span),
                    v,
                    preferred_element_type=jnp.float32,
                )
                result = summed.reshape(lh, block, DH) / norm
                out[:, j * block : (j + 1) * block, :] = result.astype(jnp.bfloat16)


def unpack_kernel(geo, map_ref, *rest):
    B, C, lh, kv_heads = geo["B"], geo["C"], geo["lh"], geo["kv_heads"]
    pieces, (out, order_ref, count_ref) = rest[:-3], rest[-3:]
    y, z = lax.axis_index("blk"), lax.axis_index("uly")
    sort_heads(map_ref, order_ref, count_ref, kv_heads)
    for db in range(B):
        for dc in range(C):
            group = lax.rem(z - dc + C, C) * B + lax.rem(y - db + B, B)
            for i in range(lh):
                h = order_ref[group * lh + i]
                out[:, pl.ds(pl.multiple_of(h * DH, DH), DH)] = pieces[db * C + dc][i]


def body(queries, keys, values, head_map, doc_lengths, plan):
    B, U = lax.axis_size("blk"), lax.axis_size("uly")
    C = U // B
    tokens, heads = queries.shape[0], head_map.shape[0]
    kv_heads = keys.shape[1] // DH
    lh = heads // U
    pieces = plan.shape[1]
    stretch = tokens * U
    block = stretch // pieces
    assert B * C == U and C % kv_heads == 0 and tokens % block == 0
    geo = dict(
        B=B, U=U, C=C, lh=lh, kv_heads=kv_heads, block=block, pieces=pieces, tokens=tokens
    )
    bf16 = jnp.bfloat16
    group_shape = jax.ShapeDtypeStruct((lh, tokens, DH), bf16)
    piece_shape = jax.ShapeDtypeStruct((2, tokens, DH), bf16)
    sort_scratch = [pltpu.SMEM((heads,), jnp.int32), pltpu.SMEM((kv_heads,), jnp.int32)]
    axes = ("blk", "uly")
    y, z = lax.axis_index("blk"), lax.axis_index("uly")

    def permute(x, target, wanted=lambda y, z: True):
        pairs = [
            (a * U + b, target(a, b)[0] * U + target(a, b)[1])
            for a in range(B)
            for b in range(U)
            if wanted(a, b)
        ]
        return lax.ppermute(x, axes, pairs)

    def limit(mib):
        return pltpu.CompilerParams(vmem_limit_bytes=mib * 1024 * 1024)

    kv_parts = pl.pallas_call(
        functools.partial(pack_kv_kernel, geo),
        out_shape=[piece_shape] * C,
        in_specs=[VMEM, VMEM],
        out_specs=[VMEM] * C,
        compiler_params=limit(4),
        name="pack_kv",
    )(keys, values)
    packed = pl.pallas_call(
        functools.partial(pack_kernel, geo),
        out_shape=[group_shape] * (B * C),
        in_specs=[SMEM, VMEM],
        out_specs=[VMEM] * (B * C),
        scratch_shapes=sort_scratch,
        compiler_params=limit(4),
        name="pack",
    )(head_map, queries)
    groups = [packed[m * C : (m + 1) * C] for m in range(B)]
    own = groups[0]

    def beside(b, j, d):
        return (b // C + j) % B * C + (b + d) % C

    kv_in = [
        permute(kv_parts[d], lambda a, b, j=j, d=d: (a, beside(b, j, d))) if j or d else kv_parts[0]
        for j in range(B)
        for d in range(C)
    ]
    crossed = [
        permute(
            groups[m][d],
            lambda a, b, m=m, d=d: ((a + m) % B, beside(b, 0, d) if a == b // C else b),
        )
        for m in range(1, B)
        for d in range(C)
    ]
    same = [own[0]] + [
        permute(own[d], lambda a, b, d=d: (a, beside(b, 0, d) if a == b // C else b))
        for d in range(1, C)
    ]
    kv_own = pl.pallas_call(
        functools.partial(gather_kv_kernel, geo),
        out_shape=jax.ShapeDtypeStruct((2, U, tokens, DH), bf16),
        in_specs=[VMEM] * U,
        out_specs=VMEM,
        compiler_params=limit(8),
        name="gather_kv",
    )(*kv_in)
    across = []
    for j in range(1, B):
        step = (y - (z // C + j)) % B
        for d in range(C):
            x = own[d]
            for m in range(1, B):
                x = jnp.where(step == m, crossed[(m - 1) * C + d], x)
            across.append(permute(x, lambda a, b, j=j, d=d: (a, beside(b, j, d))))
    kv_all = [kv_own]
    for m in range(1, B):
        kv_all.append(
            permute(
                kv_own,
                lambda a, b, m=m: ((a + m) % B, b),
                lambda a, b: B == 2 or b // C in (a, a + 1),
            )
        )

    sent = pl.pallas_call(
        functools.partial(attend_kernel, geo),
        out_shape=[group_shape] * (B * C),
        in_specs=[SMEM, SMEM] + [VMEM] * (B + C + 2 * (B - 1) * C),
        out_specs=[VMEM] * (B * C),
        scratch_shapes=[
            pltpu.VMEM((2, 2 * U, tokens, DH), bf16),
            pltpu.VMEM((U, lh, tokens, DH), bf16),
        ],
        compiler_params=limit(24),
        name="attend",
    )(doc_lengths, plan, *kv_all, *same, *crossed, *across)

    arrived = [
        permute(
            sent[db * C + dc],
            lambda a, b, db=db, dc=dc: ((a + db) % B, b // C * C + (b + dc) % C),
        )
        if db or dc
        else sent[0]
        for db in range(B)
        for dc in range(C)
    ]
    return pl.pallas_call(
        functools.partial(unpack_kernel, geo),
        out_shape=jax.ShapeDtypeStruct((tokens, heads * DH), bf16),
        in_specs=[SMEM] + [VMEM] * (B * C),
        out_specs=VMEM,
        scratch_shapes=sort_scratch,
        compiler_params=limit(4),
        name="unpack",
    )(head_map, *arrived)


def solution(mesh):
    return jax.shard_map(
        body,
        mesh=mesh,
        in_specs=(
            P(("blk", "uly"), "tp"),
            P(("blk", "uly"), "tp"),
            P(("blk", "uly"), "tp"),
            P("tp"),
            P(),
            P(),
        ),
        out_specs=P(("blk", "uly"), "tp"),
        check_vma=False,
    )
```

```python
import functools
import math

import jax
import jax.numpy as jnp
from jax import lax
from jax.experimental import pallas as pl
from jax.experimental.pallas import tpu as pltpu
from jax.sharding import PartitionSpec as P


DH = 128
LOG2E = 1.4426950408889634


VMEM = pl.BlockSpec(memory_space=pltpu.VMEM)
HBM = pl.BlockSpec(memory_space=pltpu.HBM)
SMEM = pl.BlockSpec(memory_space=pltpu.SMEM)


def sort_heads(map_ref, order_ref, count_ref, kv_heads):
    heads = map_ref.shape[0]
    per = heads // kv_heads
    for kv in range(kv_heads):
        count_ref[kv] = 0
    for h in range(heads):
        kv = map_ref[h]
        n = count_ref[kv]
        order_ref[kv * per + n] = h
        count_ref[kv] = n + 1


def pack_kv_kernel(geo, k_ref, v_ref, *rest):
    C, kv_heads = geo["C"], geo["kv_heads"]
    outs, sem = rest[:-1], rest[-1]
    z = lax.axis_index("uly")
    copies = []
    for d in range(C):
        col = pl.multiple_of(lax.rem(z + d, C) * kv_heads // C * DH, DH)
        for n, ref in enumerate((k_ref, v_ref)):
            copy = pltpu.make_async_copy(
                ref.at[:, pl.ds(col, DH)], outs[d].at[n], sem.at[d * 2 + n]
            )
            copy.start()
            copies.append(copy)
    for copy in copies:
        copy.wait()


def pack_kernel(geo, map_ref, q_ref, *rest):
    B, C, lh = geo["B"], geo["C"], geo["lh"]
    outs, (order_ref, count_ref, sem) = rest[:-3], rest[-3:]
    y, z = lax.axis_index("blk"), lax.axis_index("uly")
    sort_heads(map_ref, order_ref, count_ref, geo["kv_heads"])
    copies = []
    for m in range(B):
        for d in range(C):
            group = lax.rem(z + d, C) * B + lax.rem(y + m, B)
            for i in range(lh):
                h = order_ref[group * lh + i]
                copy = pltpu.make_async_copy(
                    q_ref.at[:, pl.ds(pl.multiple_of(h * DH, DH), DH)],
                    outs[m * C + d].at[i],
                    sem.at[(m * C + d) * lh + i],
                )
                copy.start()
                copies.append(copy)
    for copy in copies:
        copy.wait()


def gather_kv_kernel(geo, *refs):
    B, C = geo["B"], geo["C"]
    z = lax.axis_index("uly")
    out = refs[-1]
    for j in range(B):
        for d in range(C):
            source = lax.rem(z // C - j + B, B) * C + lax.rem(lax.rem(z, C) - d + C, C)
            out[0, source] = refs[j * C + d][0]
            out[1, source] = refs[j * C + d][1]


def join_kv_kernel(geo, *refs):
    B, C, U, tokens = geo["B"], geo["C"], geo["U"], geo["tokens"]
    kv_refs, kv_cat = refs[:-1], refs[-1]
    y, s = lax.axis_index("blk"), lax.axis_index("uly") // C

    @pl.when(s == 0)
    def _():
        kv_cat[:, :U] = jnp.zeros((2, U, tokens, DH), kv_cat.dtype)

    for m in range(B):
        holder = lax.rem(y - m + B, B)

        @pl.when(holder == s)
        def _():
            kv_cat[:, U:] = kv_refs[m][...]

        @pl.when(holder == s - 1)
        def _():
            kv_cat[:, :U] = kv_refs[m][...]


def join_q_kernel(geo, *refs):
    B, C = geo["B"], geo["C"]
    same, refs = refs[:C], refs[C:]
    crossed, refs = refs[: (B - 1) * C], refs[(B - 1) * C :]
    across, q_cat = refs[:-1], refs[-1]
    y, z = lax.axis_index("blk"), lax.axis_index("uly")
    s, c = z // C, lax.rem(z, C)
    for d in range(C):
        side = lax.rem(c - d + C, C)
        for j in range(1, B):
            q_cat[lax.rem(s - j + B, B) * C + side] = across[(j - 1) * C + d][...]
        for m in range(B):

            @pl.when(lax.rem(y - s + B, B) == m)
            def _():
                q_cat[s * C + side] = (same[d] if m == 0 else crossed[(m - 1) * C + d])[...]


def attend_kernel(geo, db, dc, lengths_ref, plan_ref, kv_cat, q_cat, out):
    B, C, U, lh = geo["B"], geo["C"], geo["U"], geo["lh"]
    block, pieces, tokens = geo["block"], geo["pieces"], geo["tokens"]
    stretch = tokens * U
    y, z = lax.axis_index("blk"), lax.axis_index("uly")
    s, c = z // C, lax.rem(z, C)
    ends = []
    total = 0
    for n in range(lengths_ref.shape[0]):
        total = total + lengths_ref[n]
        ends.append(total)
    per_tile = tokens // block
    span = stretch + tokens
    slots = pieces // (B * C)
    factor = LOG2E / math.sqrt(DH)
    first = lax.rem(y + db, B) * (pieces // B) + lax.rem(c + dc, C) * slots
    for j in range(slots):
        p = plan_ref[s, first + j]
        tile = p // per_tile
        inside = pl.multiple_of((p - tile * per_tile) * block, block)
        q = q_cat[tile, :, pl.ds(inside, block), :].reshape(lh * block, DH)
        k = kv_cat[0, pl.ds(tile, U + 1)].reshape(span, DH)
        v = kv_cat[1, pl.ds(tile, U + 1)].reshape(span, DH)
        score = lax.dot_general(
            q, k, (((1,), (1,)), ((), ())), preferred_element_type=jnp.float32
        )
        row = lax.broadcasted_iota(jnp.int32, (block, 1), 0)
        at = row + (s * stretch + p * block)
        start = jnp.zeros((block, 1), jnp.int32)
        for end in ends:
            start = jnp.maximum(start, jnp.where(at >= end, end, 0))
        base = (s - 1) * stretch + tile * tokens
        key = lax.broadcasted_iota(jnp.int32, (block, span), 1)
        seen = (key >= start - base) & (key <= at - base)
        score = jnp.where(seen[None], score.reshape(lh, block, span), -jnp.inf)
        top = jnp.max(score, axis=-1, keepdims=True)
        expo = jnp.exp2((score - top) * factor)
        norm = jnp.sum(expo, axis=-1, keepdims=True)
        summed = jnp.dot(
            expo.astype(jnp.bfloat16).reshape(lh * block, span),
            v,
            preferred_element_type=jnp.float32,
        )
        result = summed.reshape(lh, block, DH) / norm
        out[:, j * block : (j + 1) * block, :] = result.astype(jnp.bfloat16)


def unpack_kernel(geo, map_ref, *rest):
    B, C, lh = geo["B"], geo["C"], geo["lh"]
    pieces, (out, order_ref, count_ref, sem) = rest[:-4], rest[-4:]
    y, z = lax.axis_index("blk"), lax.axis_index("uly")
    sort_heads(map_ref, order_ref, count_ref, geo["kv_heads"])
    copies = []
    for db in range(B):
        for dc in range(C):
            group = lax.rem(z - dc + C, C) * B + lax.rem(y - db + B, B)
            for i in range(lh):
                h = order_ref[group * lh + i]
                copy = pltpu.make_async_copy(
                    pieces[db * C + dc].at[i],
                    out.at[:, pl.ds(pl.multiple_of(h * DH, DH), DH)],
                    sem.at[(db * C + dc) * lh + i],
                )
                copy.start()
                copies.append(copy)
    for copy in copies:
        copy.wait()


def body(queries, keys, values, head_map, doc_lengths, plan):
    B, U = lax.axis_size("blk"), lax.axis_size("uly")
    C = U // B
    tokens, heads = queries.shape[0], head_map.shape[0]
    kv_heads = keys.shape[1] // DH
    lh = heads // U
    pieces = plan.shape[1]
    stretch = tokens * U
    block = stretch // pieces
    assert B * C == U and C % kv_heads == 0 and tokens % block == 0
    geo = dict(
        B=B, U=U, C=C, lh=lh, kv_heads=kv_heads, block=block, pieces=pieces, tokens=tokens
    )
    bf16 = jnp.bfloat16
    group_shape = jax.ShapeDtypeStruct((lh, tokens, DH), bf16)
    piece_shape = jax.ShapeDtypeStruct((2, tokens, DH), bf16)
    sort_scratch = [pltpu.SMEM((heads,), jnp.int32), pltpu.SMEM((kv_heads,), jnp.int32)]
    axes = ("blk", "uly")
    y, z = lax.axis_index("blk"), lax.axis_index("uly")

    def permute(x, target, wanted=lambda y, z: True):
        pairs = [
            (a * U + b, target(a, b)[0] * U + target(a, b)[1])
            for a in range(B)
            for b in range(U)
            if wanted(a, b)
        ]
        return lax.ppermute(x, axes, pairs)

    def limit(mib):
        return pltpu.CompilerParams(vmem_limit_bytes=mib * 1024 * 1024)

    def call(kernel, out_shape, in_specs, args, mib, out_specs=VMEM, scratch=()):
        return pl.pallas_call(
            functools.partial(kernel, geo),
            out_shape=out_shape,
            in_specs=in_specs,
            out_specs=[out_specs] * len(out_shape) if isinstance(out_shape, list) else out_specs,
            scratch_shapes=scratch,
            compiler_params=limit(mib),
        )(*args)

    def in_hbm(x):
        return pltpu.with_memory_space_constraint(x, pltpu.HBM)

    def sent_on(x, target, wanted=lambda y, z: True):
        return permute(x, target, wanted)

    kv_parts = call(
        pack_kv_kernel,
        [piece_shape] * C,
        [HBM] * 2,
        (in_hbm(keys), in_hbm(values)),
        4,
        scratch=[pltpu.SemaphoreType.DMA((2 * C,))],
    )
    packed = call(
        pack_kernel,
        [group_shape] * (B * C),
        [SMEM, HBM],
        (head_map, in_hbm(queries)),
        4,
        scratch=[*sort_scratch, pltpu.SemaphoreType.DMA((heads,))],
    )
    groups = [packed[m * C : (m + 1) * C] for m in range(B)]
    own = groups[0]

    def beside(b, j, d):
        return (b // C + j) % B * C + (b + d) % C

    kv_in = [
        sent_on(kv_parts[d], lambda a, b, j=j, d=d: (a, beside(b, j, d)))
        if j or d
        else kv_parts[0]
        for j in range(B)
        for d in range(C)
    ]
    crossed = [
        sent_on(
            groups[m][d],
            lambda a, b, m=m, d=d: ((a + m) % B, beside(b, 0, d) if a == b // C else b),
        )
        for m in range(1, B)
        for d in range(C)
    ]
    same = [own[0]] + [
        sent_on(own[d], lambda a, b, d=d: (a, beside(b, 0, d) if a == b // C else b))
        for d in range(1, C)
    ]
    kv_own = call(
        gather_kv_kernel, jax.ShapeDtypeStruct((2, U, tokens, DH), bf16), [VMEM] * U, kv_in, 8
    )
    across = []
    for j in range(1, B):
        for d in range(C):
            x = own[d]
            for m in range(1, B):
                x = jnp.where((z // C + j + m - y) % B == 0, crossed[(m - 1) * C + d], x)
            across.append(sent_on(x, lambda a, b, j=j, d=d: (a, beside(b, j, d))))
    kv_all = [kv_own] + [
        sent_on(
            kv_own, lambda a, b, m=m: ((a + m) % B, b), lambda a, b: B == 2 or b // C in (a, a + 1)
        )
        for m in range(1, B)
    ]
    kv_cat = call(
        join_kv_kernel, jax.ShapeDtypeStruct((2, 2 * U, tokens, DH), bf16), [VMEM] * B, kv_all, 8
    )
    q_cat = call(
        join_q_kernel,
        jax.ShapeDtypeStruct((U, lh, tokens, DH), bf16),
        [VMEM] * (C + 2 * (B - 1) * C),
        (*same, *crossed, *across),
        8,
    )
    arrived = {}
    for db, dc in steps_back(B, C):
        x = call(
            lambda geo, *refs, db=db, dc=dc: attend_kernel(geo, db, dc, *refs),
            group_shape,
            [SMEM, SMEM, VMEM, VMEM],
            (doc_lengths, plan, kv_cat, q_cat),
            16,
        )
        if db or dc:
            x = sent_on(x, lambda a, b, db=db, dc=dc: ((a + db) % B, beside(b, 0, dc)))
        arrived[db, dc] = x
    return call(
        unpack_kernel,
        jax.ShapeDtypeStruct((tokens, heads * DH), bf16),
        [SMEM] + [VMEM] * (B * C),
        (head_map, *(arrived[db, dc] for db in range(B) for dc in range(C))),
        4,
        out_specs=HBM,
        scratch=[*sort_scratch, pltpu.SemaphoreType.DMA((heads,))],
    )


def steps_back(B, C):
    return [(db, dc) for db in reversed(range(B)) for dc in reversed(range(C))]


def solution(mesh):
    return jax.shard_map(
        body,
        mesh=mesh,
        in_specs=(
            P(("blk", "uly"), "tp"),
            P(("blk", "uly"), "tp"),
            P(("blk", "uly"), "tp"),
            P("tp"),
            P(),
            P(),
        ),
        out_specs=P(("blk", "uly"), "tp"),
        check_vma=False,
    )
```

```python
import functools
import math

import jax
import jax.numpy as jnp
from jax import lax
from jax.experimental import pallas as pl
from jax.experimental.pallas import tpu as pltpu
from jax.sharding import PartitionSpec as P


DH = 128
LOG2E = 1.4426950408889634


VMEM = pl.BlockSpec(memory_space=pltpu.VMEM)
HBM = pl.BlockSpec(memory_space=pltpu.HBM)
SMEM = pl.BlockSpec(memory_space=pltpu.SMEM)


def sort_heads(map_ref, order_ref, kv_heads):
    heads = map_ref.shape[0]
    per = heads // kv_heads
    place = [kv * per for kv in range(kv_heads)]
    for h in range(heads):
        kv = map_ref[h]
        at = place[0]
        for n in range(1, kv_heads):
            at = jnp.where(kv == n, place[n], at)
        order_ref[at] = h
        place = [p + (kv == n).astype(jnp.int32) for n, p in enumerate(place)]


def pack_kernel(geo, steps, map_ref, q_ref, *rest):
    B, C, lh = geo["B"], geo["C"], geo["lh"]
    outs, (order_ref, sem) = rest[:-2], rest[-2:]
    y, z = lax.axis_index("blk"), lax.axis_index("uly")
    sort_heads(map_ref, order_ref, geo["kv_heads"])
    copies = []
    for n, (m, d) in enumerate(steps):
        group = lax.rem(z + d, C) * B + lax.rem(y + m, B)
        for i in range(lh):
            h = order_ref[group * lh + i]
            copy = pltpu.make_async_copy(
                q_ref.at[:, pl.ds(pl.multiple_of(h * DH, DH), DH)],
                outs[n].at[i],
                sem.at[n * lh + i],
            )
            copy.start()
            copies.append(copy)
    for copy in copies:
        copy.wait()


def pick_kv_kernel(geo, *refs):
    B, C, kv_heads = geo["B"], geo["C"], geo["kv_heads"]
    k_refs, v_refs, outs = refs[:B], refs[B : 2 * B], refs[2 * B :]
    z = lax.axis_index("uly")
    for d in range(C):
        col = pl.multiple_of(lax.rem(z + d, C) * kv_heads // C * DH, DH)
        for j in range(B):
            outs[d][0, j] = k_refs[j][:, pl.ds(col, DH)]
            outs[d][1, j] = v_refs[j][:, pl.ds(col, DH)]


def gather_kv_kernel(geo, *refs):
    B, C = geo["B"], geo["C"]
    z = lax.axis_index("uly")
    out = refs[-1]
    for j in range(B):
        for d in range(C):
            source = lax.rem(z // C - j + B, B) * C + lax.rem(lax.rem(z, C) - d + C, C)
            out[0, source] = refs[d][0, j]
            out[1, source] = refs[d][1, j]


def join_kv_kernel(geo, *refs):
    B, C, U, tokens = geo["B"], geo["C"], geo["U"], geo["tokens"]
    kv_refs, kv_cat = refs[:-1], refs[-1]
    y, s = lax.axis_index("blk"), lax.axis_index("uly") // C

    @pl.when(s == 0)
    def _():
        kv_cat[:, :U] = jnp.zeros((2, U, tokens, DH), kv_cat.dtype)

    for m in range(B):
        holder = lax.rem(y - m + B, B)

        @pl.when(holder == s)
        def _():
            kv_cat[:, U:] = kv_refs[m][...]

        @pl.when(holder == s - 1)
        def _():
            kv_cat[:, :U] = kv_refs[m][...]


def join_q_kernel(geo, *refs):
    B, C = geo["B"], geo["C"]
    across, q_cat = refs[:-1], refs[-1]
    z = lax.axis_index("uly")
    for j in range(B):
        for d in range(C):
            source = lax.rem(z // C - j + B, B) * C + lax.rem(lax.rem(z, C) - d + C, C)
            q_cat[source] = across[j * C + d][...]


def attend_kernel(geo, db, places, lengths_ref, plan_ref, kv_cat, q_cat, *outs):
    B, C, U, lh = geo["B"], geo["C"], geo["U"], geo["lh"]
    block, pieces, tokens = geo["block"], geo["pieces"], geo["tokens"]
    stretch = tokens * U
    y, z = lax.axis_index("blk"), lax.axis_index("uly")
    s, c = z // C, lax.rem(z, C)
    ends = []
    total = 0
    for n in range(lengths_ref.shape[0]):
        total = total + lengths_ref[n]
        ends.append(total)
    per_tile = tokens // block
    span = stretch + tokens
    slots = pieces // (B * C)
    factor = LOG2E / math.sqrt(DH)
    row = lax.broadcasted_iota(jnp.int32, (block, 1), 0)
    key = lax.broadcasted_iota(jnp.int32, (block, span), 1)
    for out, dc in zip(outs, places):
        first = lax.rem(y + db, B) * (pieces // B) + lax.rem(c + dc, C) * slots
        for j in range(slots):
            p = plan_ref[s, first + j]
            tile = p // per_tile
            inside = pl.multiple_of((p - tile * per_tile) * block, block)
            q = q_cat[tile, :, pl.ds(inside, block), :].reshape(lh * block, DH)
            k = kv_cat[0, pl.ds(tile, U + 1)].reshape(span, DH)
            v = kv_cat[1, pl.ds(tile, U + 1)].reshape(span, DH)
            score = lax.dot_general(
                q, k, (((1,), (1,)), ((), ())), preferred_element_type=jnp.float32
            )
            at = row + (s * stretch + p * block)
            start = jnp.zeros((block, 1), jnp.int32)
            for end in ends:
                start = jnp.where(at >= end, end, start)
            base = (s - 1) * stretch + tile * tokens
            seen = (key >= start - base) & (key <= at - base)
            score = jnp.where(seen[None], score.reshape(lh, block, span), -jnp.inf)
            top = jnp.max(score, axis=-1, keepdims=True)
            expo = jnp.exp2((score - top) * factor)
            norm = jnp.sum(expo, axis=-1, keepdims=True)
            summed = jnp.dot(
                expo.astype(jnp.bfloat16).reshape(lh * block, span),
                v,
                preferred_element_type=jnp.float32,
            )
            result = summed.reshape(lh, block, DH) / norm
            out[:, j * block : (j + 1) * block, :] = result.astype(jnp.bfloat16)


def unpack_kernel(geo, map_ref, *rest):
    B, C, lh = geo["B"], geo["C"], geo["lh"]
    pieces, (out, order_ref, sem) = rest[:-3], rest[-3:]
    y, z = lax.axis_index("blk"), lax.axis_index("uly")
    sort_heads(map_ref, order_ref, geo["kv_heads"])
    copies = []
    for db in range(B):
        for dc in range(C):
            group = lax.rem(z - dc + C, C) * B + lax.rem(y - db + B, B)
            for i in range(lh):
                h = order_ref[group * lh + i]
                copy = pltpu.make_async_copy(
                    pieces[db * C + dc].at[i],
                    out.at[:, pl.ds(pl.multiple_of(h * DH, DH), DH)],
                    sem.at[(db * C + dc) * lh + i],
                )
                copy.start()
                copies.append(copy)
    for copy in copies:
        copy.wait()


def body(queries, keys, values, head_map, doc_lengths, plan):
    B, U = lax.axis_size("blk"), lax.axis_size("uly")
    C = U // B
    tokens, heads = queries.shape[0], head_map.shape[0]
    kv_heads = keys.shape[1] // DH
    lh = heads // U
    pieces = plan.shape[1]
    stretch = tokens * U
    block = stretch // pieces
    assert B * C == U and C % kv_heads == 0 and tokens % block == 0
    geo = dict(
        B=B, U=U, C=C, lh=lh, kv_heads=kv_heads, block=block, pieces=pieces, tokens=tokens
    )
    bf16 = jnp.bfloat16
    group_shape = jax.ShapeDtypeStruct((lh, tokens, DH), bf16)
    piece_shape = jax.ShapeDtypeStruct((2, B, tokens, DH), bf16)
    sort_scratch = [pltpu.SMEM((heads,), jnp.int32)]
    axes = ("blk", "uly")
    y, z = lax.axis_index("blk"), lax.axis_index("uly")

    def permute(x, target, wanted=lambda y, z: True):
        pairs = [
            (a * U + b, target(a, b)[0] * U + target(a, b)[1])
            for a in range(B)
            for b in range(U)
            if wanted(a, b)
        ]
        return lax.ppermute(x, axes, pairs)

    def limit(mib):
        return pltpu.CompilerParams(vmem_limit_bytes=mib * 1024 * 1024)

    def call(kernel, out_shape, in_specs, args, mib, out_specs=VMEM, scratch=()):
        return pl.pallas_call(
            functools.partial(kernel, geo),
            out_shape=out_shape,
            in_specs=in_specs,
            out_specs=[out_specs] * len(out_shape) if isinstance(out_shape, list) else out_specs,
            scratch_shapes=scratch,
            compiler_params=limit(mib),
        )(*args)

    def in_hbm(x):
        return pltpu.with_memory_space_constraint(x, pltpu.HBM)

    def sent_on(x, target, wanted=lambda y, z: True):
        return permute(x, target, wanted)

    def beside(b, j, d):
        return (b // C + j) % B * C + (b + d) % C

    k_in, v_in = [
        [x]
        + [sent_on(x, lambda a, b, j=j: (a, beside(b, j, 0))) for j in range(1, B)]
        for x in (keys, values)
    ]
    steps = [(m, d) for m in range(B) for d in range(C)]
    packed = call(
        lambda geo, *refs: pack_kernel(geo, steps, *refs),
        [group_shape] * len(steps),
        [SMEM, HBM],
        (head_map, in_hbm(queries)),
        4,
        scratch=[*sort_scratch, pltpu.SemaphoreType.DMA((heads,))],
    )
    groups = dict(zip(steps, packed))
    own = [groups[0, d] for d in range(C)]

    crossed = [
        sent_on(groups[m, d], lambda a, b, m=m: ((a + m) % B, b))
        for m in range(1, B)
        for d in range(C)
    ]
    picked = call(pick_kv_kernel, [piece_shape] * C, [VMEM] * (2 * B), (*k_in, *v_in), 4)
    kv_own = call(
        gather_kv_kernel,
        jax.ShapeDtypeStruct((2, U, tokens, DH), bf16),
        [VMEM] * C,
        [picked[0]]
        + [sent_on(picked[d], lambda a, b, d=d: (a, beside(b, 0, d))) for d in range(1, C)],
        8,
    )
    across = []
    for j in range(B):
        for d in range(C):
            x = own[d]
            for m in range(1, B):
                x = jnp.where((z // C + j + m - y) % B == 0, crossed[(m - 1) * C + d], x)
            if j or d:
                x = sent_on(x, lambda a, b, j=j, d=d: (a, beside(b, j, d)))
            across.append(x)
    kv_all = [kv_own] + [
        sent_on(
            kv_own, lambda a, b, m=m: ((a + m) % B, b), lambda a, b: B == 2 or b // C in (a, a + 1)
        )
        for m in range(1, B)
    ]
    kv_cat = call(
        join_kv_kernel, jax.ShapeDtypeStruct((2, 2 * U, tokens, DH), bf16), [VMEM] * B, kv_all, 8
    )
    q_cat = call(
        join_q_kernel, jax.ShapeDtypeStruct((U, lh, tokens, DH), bf16), [VMEM] * U, across, 8
    )
    arrived = {}
    places = steps_back(C)
    for db in steps_back(B):
        results = call(
            lambda geo, *refs, db=db: attend_kernel(geo, db, places, *refs),
            [group_shape] * C,
            [SMEM, SMEM, VMEM, VMEM],
            (doc_lengths, plan, kv_cat, q_cat),
            16,
        )
        for dc, x in zip(places, results):
            if db or dc:
                x = sent_on(x, lambda a, b, db=db, dc=dc: ((a + db) % B, beside(b, 0, dc)))
            arrived[db, dc] = x
    return call(
        unpack_kernel,
        jax.ShapeDtypeStruct((tokens, heads * DH), bf16),
        [SMEM] + [VMEM] * (B * C),
        (head_map, *(arrived[db, dc] for db in range(B) for dc in range(C))),
        4,
        out_specs=HBM,
        scratch=[*sort_scratch, pltpu.SemaphoreType.DMA((heads,))],
    )


def steps_back(n):
    return list(reversed(range(n)))


def solution(mesh):
    return jax.shard_map(
        body,
        mesh=mesh,
        in_specs=(
            P(("blk", "uly"), "tp"),
            P(("blk", "uly"), "tp"),
            P(("blk", "uly"), "tp"),
            P("tp"),
            P(),
            P(),
        ),
        out_specs=P(("blk", "uly"), "tp"),
        check_vma=False,
    )
```

```python
import functools
import math

import jax
import jax.numpy as jnp
from jax import lax
from jax.experimental import pallas as pl
from jax.experimental.pallas import tpu as pltpu
from jax.sharding import PartitionSpec as P


DH = 128
LOG2E = 1.4426950408889634


VMEM = pl.BlockSpec(memory_space=pltpu.VMEM)
HBM = pl.BlockSpec(memory_space=pltpu.HBM)
SMEM = pl.BlockSpec(memory_space=pltpu.SMEM)


def sort_heads(map_ref, order_ref, kv_heads):
    heads = map_ref.shape[0]
    per = heads // kv_heads
    place = [kv * per for kv in range(kv_heads)]
    for h in range(heads):
        kv = map_ref[h]
        at = place[0]
        for n in range(1, kv_heads):
            at = jnp.where(kv == n, place[n], at)
        order_ref[at] = h
        place = [p + (kv == n).astype(jnp.int32) for n, p in enumerate(place)]


def pack_kernel(geo, map_hbm, q_hbm, k_hbm, v_hbm, *rest):
    B, C, lh, kv_heads = geo["B"], geo["C"], geo["lh"], geo["kv_heads"]
    outs, (map_ref, q_ref, order_ref, sem) = rest[:-4], rest[-4:]
    y, z = lax.axis_index("blk"), lax.axis_index("uly")
    copies = [
        pltpu.make_async_copy(map_hbm, map_ref, sem.at[0]),
        pltpu.make_async_copy(q_hbm, q_ref, sem.at[1]),
    ]
    for d in range(C):
        col = pl.multiple_of(lax.rem(z + d, C) * kv_heads // C * DH, DH)
        for n, ref in enumerate((k_hbm, v_hbm)):
            copies.append(
                pltpu.make_async_copy(
                    ref.at[:, pl.ds(col, DH)], outs[B * C + d].at[n], sem.at[2 + d * 2 + n]
                )
            )
    for copy in copies:
        copy.start()
    copies[0].wait()
    sort_heads(map_ref, order_ref, kv_heads)
    copies[1].wait()
    for m in range(B):
        for d in range(C):
            group = lax.rem(z + d, C) * B + lax.rem(y + m, B)
            for i in range(lh):
                h = order_ref[group * lh + i]
                outs[m * C + d][i] = q_ref[:, pl.ds(pl.multiple_of(h * DH, DH), DH)]
    for copy in copies[2:]:
        copy.wait()


def gather_kv_kernel(geo, *refs):
    B, C = geo["B"], geo["C"]
    z = lax.axis_index("uly")
    out = refs[-1]
    for j in range(B):
        for d in range(C):
            source = lax.rem(z // C - j + B, B) * C + lax.rem(lax.rem(z, C) - d + C, C)
            out[0, source] = refs[j * C + d][0]
            out[1, source] = refs[j * C + d][1]


def document_ends(lengths_ref):
    ends = []
    total = 0
    for n in range(lengths_ref.shape[0]):
        total = total + lengths_ref[n]
        ends.append(total)
    return ends


def attend_tile(geo, ends, kv_cat, q_ref, out_ref, at_out, tile):
    C, U, lh, tokens = geo["C"], geo["U"], geo["lh"], geo["tokens"]
    stretch = tokens * U
    s = lax.axis_index("uly") // C
    factor = LOG2E / math.sqrt(DH)
    grain = -(-(U + 1) // 5)
    widths = [*range(grain, U + 1, grain), U + 1]
    row = lax.broadcasted_iota(jnp.int32, (tokens, 1), 0)
    first = s * stretch + tile * tokens
    begin = 0
    for end in ends:
        begin = jnp.where(first >= end, end, begin)
    needed = s * U + tile - begin // tokens + 1
    at = row + first
    start = jnp.zeros((tokens, 1), jnp.int32)
    for end in ends:
        start = jnp.where(at >= end, end, start)

    def with_keys(width):
        low = tile + U + 1 - width
        span = width * tokens
        q = q_ref[...].reshape(lh * tokens, DH)
        k = kv_cat[0, pl.ds(low, width)].reshape(span, DH)
        v = kv_cat[1, pl.ds(low, width)].reshape(span, DH)
        score = lax.dot_general(
            q, k, (((1,), (1,)), ((), ())), preferred_element_type=jnp.float32
        )
        base = (s - 1) * stretch + low * tokens
        key = lax.broadcasted_iota(jnp.int32, (tokens, span), 1)
        seen = (key >= start - base) & (key <= at - base)
        score = jnp.where(seen[None], score.reshape(lh, tokens, span), -jnp.inf)
        top = jnp.max(score, axis=-1, keepdims=True)
        expo = jnp.exp2((score - top) * factor)
        norm = jnp.sum(expo, axis=-1, keepdims=True)
        summed = jnp.dot(
            expo.astype(jnp.bfloat16).reshape(lh * tokens, span),
            v,
            preferred_element_type=jnp.float32,
        )
        out_ref[at_out] = (summed.reshape(lh, tokens, DH) / norm).astype(jnp.bfloat16)

    less = 0
    for width in widths:
        fits = needed > less
        if width < U + 1:
            fits = fits & (needed <= width)
        pl.when(fits)(functools.partial(with_keys, width))
        less = width


def tile_of(geo, step):
    B, C = geo["B"], geo["C"]
    z = lax.axis_index("uly")
    return lax.rem(z // C - step[0] + B, B) * C + lax.rem(lax.rem(z, C) - step[1] + C, C)


def attend_early_kernel(geo, early, lengths_hbm, *refs):
    B, C, U, tokens = geo["B"], geo["C"], geo["U"], geo["tokens"]
    kv_refs, refs = refs[:B], refs[B:]
    rows, (kv_cat, done, lengths_ref, sem) = refs[:-4], refs[-4:]
    y, s = lax.axis_index("blk"), lax.axis_index("uly") // C
    table = pltpu.make_async_copy(lengths_hbm, lengths_ref, sem.at[0])
    table.start()

    @pl.when(s == 0)
    def _():
        kv_cat[:, :U] = jnp.zeros((2, U, tokens, DH), kv_cat.dtype)

    for m in range(B):
        holder = lax.rem(y - m + B, B)

        @pl.when(holder == s)
        def _():
            kv_cat[:, U:] = kv_refs[m][...]

        @pl.when(holder == s - 1)
        def _():
            kv_cat[:, :U] = kv_refs[m][...]

    table.wait()
    ends = document_ends(lengths_ref)
    for n, step in enumerate(early):
        attend_tile(geo, ends, kv_cat, rows[n], done, n, tile_of(geo, step))


def attend_late_kernel(geo, early, late, steps, lengths_hbm, plan_hbm, kv_cat, done, *refs):
    B, C = geo["B"], geo["C"]
    block, pieces, tokens = geo["block"], geo["pieces"], geo["tokens"]
    rows, refs = refs[: len(late)], refs[len(late) :]
    outs, (lengths_ref, plan_ref, all_done, sem) = refs[:-4], refs[-4:]
    y, z = lax.axis_index("blk"), lax.axis_index("uly")
    s, c = z // C, lax.rem(z, C)
    tables = [
        pltpu.make_async_copy(lengths_hbm, lengths_ref, sem.at[0]),
        pltpu.make_async_copy(plan_hbm, plan_ref, sem.at[1]),
    ]
    for table in tables:
        table.start()
    for n, step in enumerate(early):
        all_done[tile_of(geo, step)] = done[n]
    for table in tables:
        table.wait()
    ends = document_ends(lengths_ref)
    for n, step in enumerate(late):
        tile = tile_of(geo, step)
        attend_tile(geo, ends, kv_cat, rows[n], all_done, tile, tile)
    per_tile = tokens // block
    slots = pieces // (B * C)
    for out, (db, dc) in zip(outs, steps):
        slot = lax.rem(y + db, B) * (pieces // B) + lax.rem(c + dc, C) * slots
        for j in range(slots):
            p = plan_ref[s, slot + j]
            tile = p // per_tile
            inside = pl.multiple_of((p - tile * per_tile) * block, block)
            out[:, j * block : (j + 1) * block, :] = all_done[tile, :, pl.ds(inside, block), :]


def unpack_kernel(geo, map_ref, *rest):
    B, C, lh = geo["B"], geo["C"], geo["lh"]
    pieces, (out, order_ref, sem) = rest[:-3], rest[-3:]
    y, z = lax.axis_index("blk"), lax.axis_index("uly")
    sort_heads(map_ref, order_ref, geo["kv_heads"])
    copies = []
    for db in range(B):
        for dc in range(C):
            group = lax.rem(z - dc + C, C) * B + lax.rem(y - db + B, B)
            for i in range(lh):
                h = order_ref[group * lh + i]
                copy = pltpu.make_async_copy(
                    pieces[db * C + dc].at[i],
                    out.at[:, pl.ds(pl.multiple_of(h * DH, DH), DH)],
                    sem.at[(db * C + dc) * lh + i],
                )
                copy.start()
                copies.append(copy)
    for copy in copies:
        copy.wait()


def body(queries, keys, values, head_map, doc_lengths, plan):
    B, U = lax.axis_size("blk"), lax.axis_size("uly")
    C = U // B
    tokens, heads = queries.shape[0], head_map.shape[0]
    kv_heads = keys.shape[1] // DH
    lh = heads // U
    pieces = plan.shape[1]
    stretch = tokens * U
    block = stretch // pieces
    assert B * C == U and C % kv_heads == 0 and tokens % block == 0
    geo = dict(
        B=B, U=U, C=C, lh=lh, kv_heads=kv_heads, block=block, pieces=pieces, tokens=tokens
    )
    bf16 = jnp.bfloat16
    group_shape = jax.ShapeDtypeStruct((lh, tokens, DH), bf16)
    piece_shape = jax.ShapeDtypeStruct((2, tokens, DH), bf16)
    sort_scratch = [pltpu.SMEM((heads,), jnp.int32)]
    axes = ("blk", "uly")
    y, z = lax.axis_index("blk"), lax.axis_index("uly")

    def permute(x, target, wanted=lambda y, z: True):
        pairs = [
            (a * U + b, target(a, b)[0] * U + target(a, b)[1])
            for a in range(B)
            for b in range(U)
            if wanted(a, b)
        ]
        return lax.ppermute(x, axes, pairs)

    def limit(mib):
        return pltpu.CompilerParams(vmem_limit_bytes=mib * 1024 * 1024)

    def call(kernel, out_shape, in_specs, args, mib, out_specs=VMEM, scratch=()):
        return pl.pallas_call(
            functools.partial(kernel, geo),
            out_shape=out_shape,
            in_specs=in_specs,
            out_specs=[out_specs] * len(out_shape) if isinstance(out_shape, list) else out_specs,
            scratch_shapes=scratch,
            compiler_params=limit(mib),
        )(*args)

    def in_hbm(x):
        return pltpu.with_memory_space_constraint(x, pltpu.HBM)

    def sent_on(x, target, wanted=lambda y, z: True):
        return permute(x, target, wanted)

    def beside(b, j, d):
        return (b // C + j) % B * C + (b + d) % C

    steps = [(m, d) for m in range(B) for d in range(C)]
    packed = call(
        pack_kernel,
        [group_shape] * (B * C) + [piece_shape] * C,
        [HBM] * 4,
        tuple(in_hbm(x) for x in (head_map, queries, keys, values)),
        6,
        scratch=[
            pltpu.SMEM((heads,), jnp.int32),
            pltpu.VMEM((tokens, heads * DH), bf16),
            *sort_scratch,
            pltpu.SemaphoreType.DMA((2 + 2 * C,)),
        ],
    )
    groups, kv_parts = dict(zip(steps, packed)), packed[B * C :]
    own = [groups[0, d] for d in range(C)]
    kv_in = [
        sent_on(kv_parts[d], lambda a, b, j=j, d=d: (a, beside(b, j, d)))
        if j or d
        else kv_parts[0]
        for j in range(B)
        for d in range(C)
    ]
    crossed = [
        sent_on(groups[m, d], lambda a, b, m=m: ((a + m) % B, b))
        for m in range(1, B)
        for d in range(C)
    ]
    kv_own = call(
        gather_kv_kernel, jax.ShapeDtypeStruct((2, U, tokens, DH), bf16), [VMEM] * U, kv_in, 8
    )
    across = []
    for j in range(B):
        for d in range(C):
            x = own[d]
            for m in range(1, B):
                x = jnp.where((z // C + j + m - y) % B == 0, crossed[(m - 1) * C + d], x)
            if j or d:
                x = sent_on(x, lambda a, b, j=j, d=d: (a, beside(b, j, d)))
            across.append(x)
    kv_all = [kv_own] + [
        sent_on(
            kv_own, lambda a, b, m=m: ((a + m) % B, b), lambda a, b: B == 2 or b // C in (a, a + 1)
        )
        for m in range(1, B)
    ]
    early, late = arrivals(B, C)
    tiles = [(j, d) for j in range(B) for d in range(C)]
    lengths_table = pltpu.SMEM(doc_lengths.shape, jnp.int32)
    kv_cat, done = call(
        lambda geo, *refs: attend_early_kernel(geo, early, *refs),
        [
            jax.ShapeDtypeStruct((2, 2 * U, tokens, DH), bf16),
            jax.ShapeDtypeStruct((len(early), lh, tokens, DH), bf16),
        ],
        [HBM] + [VMEM] * (B + len(early)),
        (in_hbm(doc_lengths), *kv_all, *(across[tiles.index(step)] for step in early)),
        16,
        scratch=[lengths_table, pltpu.SemaphoreType.DMA((1,))],
    )
    steps = [(db, dc) for db in reversed(range(B)) for dc in reversed(range(C))]
    results = call(
        lambda geo, *refs: attend_late_kernel(geo, early, late, steps, *refs),
        [group_shape] * len(steps),
        [HBM, HBM] + [VMEM] * (2 + len(late)),
        (
            in_hbm(doc_lengths),
            in_hbm(plan),
            kv_cat,
            done,
            *(across[tiles.index(step)] for step in late),
        ),
        16,
        scratch=[
            lengths_table,
            pltpu.SMEM(plan.shape, jnp.int32),
            pltpu.VMEM((U, lh, tokens, DH), bf16),
            pltpu.SemaphoreType.DMA((2,)),
        ],
    )
    arrived = {}
    for (db, dc), x in zip(steps, results):
        if db or dc:
            x = sent_on(x, lambda a, b, db=db, dc=dc: ((a + db) % B, beside(b, 0, dc)))
        arrived[db, dc] = x
    return call(
        unpack_kernel,
        jax.ShapeDtypeStruct((tokens, heads * DH), bf16),
        [SMEM] + [VMEM] * (B * C),
        (head_map, *(arrived[db, dc] for db in range(B) for dc in range(C))),
        4,
        out_specs=HBM,
        scratch=[*sort_scratch, pltpu.SemaphoreType.DMA((heads,))],
    )


def arrivals(B, C):
    tiles = [(j, d) for j in range(B) for d in range(C)]
    late = [step for step in tiles if step[0] and step[1]]
    return [step for step in tiles if step not in late], late


def solution(mesh):
    return jax.shard_map(
        body,
        mesh=mesh,
        in_specs=(
            P(("blk", "uly"), "tp"),
            P(("blk", "uly"), "tp"),
            P(("blk", "uly"), "tp"),
            P("tp"),
            P(),
            P(),
        ),
        out_specs=P(("blk", "uly"), "tp"),
        check_vma=False,
    )
```

```python
import functools
import math

import jax
import jax.numpy as jnp
from jax import lax
from jax.experimental import pallas as pl
from jax.experimental.pallas import tpu as pltpu
from jax.sharding import PartitionSpec as P


DH = 128
LOG2E = 1.4426950408889634


VMEM = pl.BlockSpec(memory_space=pltpu.VMEM)
HBM = pl.BlockSpec(memory_space=pltpu.HBM)


def sort_heads(map_ref, order_ref, kv_heads):
    heads = map_ref.shape[1]
    per = heads // kv_heads
    place = [kv * per for kv in range(kv_heads)]
    for h in range(heads):
        kv = map_ref[0, h]
        at = place[0]
        for n in range(1, kv_heads):
            at = jnp.where(kv == n, place[n], at)
        order_ref[at] = h
        place = [p + (kv == n).astype(jnp.int32) for n, p in enumerate(place)]


def pack_kernel(geo, map_hbm, q_hbm, k_hbm, v_hbm, lengths_hbm, *rest):
    B, C, lh, kv_heads = geo["B"], geo["C"], geo["lh"], geo["kv_heads"]
    outs, (map_ref, q_ref, order_ref, sem) = rest[:-4], rest[-4:]
    y, z = lax.axis_index("blk"), lax.axis_index("uly")
    copies = [
        pltpu.make_async_copy(map_hbm, map_ref, sem.at[0]),
        pltpu.make_async_copy(q_hbm, q_ref, sem.at[1]),
        pltpu.make_async_copy(map_hbm, outs[-2], sem.at[2]),
        pltpu.make_async_copy(lengths_hbm, outs[-1], sem.at[3]),
    ]
    for d in range(C):
        col = pl.multiple_of(lax.rem(z + d, C) * kv_heads // C * DH, DH)
        for n, ref in enumerate((k_hbm, v_hbm)):
            copies.append(
                pltpu.make_async_copy(
                    ref.at[:, pl.ds(col, DH)], outs[B * C + d].at[n], sem.at[4 + d * 2 + n]
                )
            )
    for copy in copies:
        copy.start()
    copies[0].wait()
    sort_heads(map_ref, order_ref, kv_heads)
    copies[1].wait()
    for m in range(B):
        for d in range(C):
            group = lax.rem(z + d, C) * B + lax.rem(y + m, B)
            for i in range(lh):
                h = order_ref[group * lh + i]
                outs[m * C + d][i] = q_ref[:, pl.ds(pl.multiple_of(h * DH, DH), DH)]
    for copy in copies[2:]:
        copy.wait()


def gather_kv_kernel(geo, *refs):
    B, C = geo["B"], geo["C"]
    z = lax.axis_index("uly")
    out = refs[-1]
    for j in range(B):
        for d in range(C):
            source = lax.rem(z // C - j + B, B) * C + lax.rem(lax.rem(z, C) - d + C, C)
            out[0, source] = refs[j * C + d][0]
            out[1, source] = refs[j * C + d][1]


def document_ends(lengths_ref):
    ends = []
    total = 0
    for n in range(lengths_ref.shape[1]):
        total = total + lengths_ref[0, n]
        ends.append(total)
    return ends


def attend_tile(geo, ends, kv_cat, q_ref, out_ref, at_out, tile):
    C, U, lh, tokens = geo["C"], geo["U"], geo["lh"], geo["tokens"]
    stretch = tokens * U
    s = lax.axis_index("uly") // C
    factor = LOG2E / math.sqrt(DH)
    grain = -(-(U + 1) // 5)
    widths = [*range(grain, U + 1, grain), U + 1]
    row = lax.broadcasted_iota(jnp.int32, (tokens, 1), 0)
    first = s * stretch + tile * tokens
    begin = 0
    for end in ends:
        begin = jnp.where(first >= end, end, begin)
    needed = s * U + tile - begin // tokens + 1
    at = row + first
    start = jnp.zeros((tokens, 1), jnp.int32)
    for end in ends:
        start = jnp.where(at >= end, end, start)

    def with_keys(width):
        low = tile + U + 1 - width
        span = width * tokens
        q = q_ref[...].reshape(lh * tokens, DH)
        k = kv_cat[0, pl.ds(low, width)].reshape(span, DH)
        v = kv_cat[1, pl.ds(low, width)].reshape(span, DH)
        score = lax.dot_general(
            q, k, (((1,), (1,)), ((), ())), preferred_element_type=jnp.float32
        )
        base = (s - 1) * stretch + low * tokens
        key = lax.broadcasted_iota(jnp.int32, (tokens, span), 1)
        seen = (key >= start - base) & (key <= at - base)
        score = jnp.where(seen[None], score.reshape(lh, tokens, span), -jnp.inf)
        top = jnp.max(score, axis=-1, keepdims=True)
        expo = jnp.exp2((score - top) * factor)
        norm = jnp.sum(expo, axis=-1, keepdims=True)
        summed = jnp.dot(
            expo.astype(jnp.bfloat16).reshape(lh * tokens, span),
            v,
            preferred_element_type=jnp.float32,
        )
        out_ref[at_out] = (summed.reshape(lh, tokens, DH) / norm).astype(jnp.bfloat16)

    less = 0
    for width in widths:
        fits = needed > less
        if width < U + 1:
            fits = fits & (needed <= width)
        pl.when(fits)(functools.partial(with_keys, width))
        less = width


def tile_of(geo, step):
    B, C = geo["B"], geo["C"]
    z = lax.axis_index("uly")
    return lax.rem(z // C - step[0] + B, B) * C + lax.rem(lax.rem(z, C) - step[1] + C, C)


def attend_early_kernel(geo, early, lengths_ref, *refs):
    B, C, U, tokens = geo["B"], geo["C"], geo["U"], geo["tokens"]
    kv_refs, refs = refs[:B], refs[B:]
    rows, (kv_cat, done) = refs[:-2], refs[-2:]
    y, s = lax.axis_index("blk"), lax.axis_index("uly") // C

    @pl.when(s == 0)
    def _():
        kv_cat[:, :U] = jnp.zeros((2, U, tokens, DH), kv_cat.dtype)

    for m in range(B):
        holder = lax.rem(y - m + B, B)

        @pl.when(holder == s)
        def _():
            kv_cat[:, U:] = kv_refs[m][...]

        @pl.when(holder == s - 1)
        def _():
            kv_cat[:, :U] = kv_refs[m][...]

    ends = document_ends(lengths_ref)
    for n, step in enumerate(early):
        attend_tile(geo, ends, kv_cat, rows[n], done, n, tile_of(geo, step))


def attend_late_kernel(geo, early, late, steps, plan_hbm, lengths_ref, kv_cat, done, *refs):
    B, C = geo["B"], geo["C"]
    block, pieces, tokens = geo["block"], geo["pieces"], geo["tokens"]
    rows, refs = refs[: len(late)], refs[len(late) :]
    outs, (plan_ref, all_done, sem) = refs[:-3], refs[-3:]
    y, z = lax.axis_index("blk"), lax.axis_index("uly")
    s, c = z // C, lax.rem(z, C)
    table = pltpu.make_async_copy(plan_hbm, plan_ref, sem.at[0])
    table.start()
    for n, step in enumerate(early):
        all_done[tile_of(geo, step)] = done[n]
    ends = document_ends(lengths_ref)
    for n, step in enumerate(late):
        tile = tile_of(geo, step)
        attend_tile(geo, ends, kv_cat, rows[n], all_done, tile, tile)
    table.wait()
    per_tile = tokens // block
    slots = pieces // (B * C)
    for out, (db, dc) in zip(outs, steps):
        slot = lax.rem(y + db, B) * (pieces // B) + lax.rem(c + dc, C) * slots
        for j in range(slots):
            p = plan_ref[s, slot + j]
            tile = p // per_tile
            inside = pl.multiple_of((p - tile * per_tile) * block, block)
            out[:, j * block : (j + 1) * block, :] = all_done[tile, :, pl.ds(inside, block), :]


def unpack_kernel(geo, map_ref, *rest):
    B, C, lh = geo["B"], geo["C"], geo["lh"]
    pieces, (out, order_ref, sem) = rest[:-3], rest[-3:]
    y, z = lax.axis_index("blk"), lax.axis_index("uly")
    sort_heads(map_ref, order_ref, geo["kv_heads"])
    copies = []
    for db in range(B):
        for dc in range(C):
            group = lax.rem(z - dc + C, C) * B + lax.rem(y - db + B, B)
            for i in range(lh):
                h = order_ref[group * lh + i]
                copy = pltpu.make_async_copy(
                    pieces[db * C + dc].at[i],
                    out.at[:, pl.ds(pl.multiple_of(h * DH, DH), DH)],
                    sem.at[(db * C + dc) * lh + i],
                )
                copy.start()
                copies.append(copy)
    for copy in copies:
        copy.wait()


def body(queries, keys, values, head_map, doc_lengths, plan):
    B, U = lax.axis_size("blk"), lax.axis_size("uly")
    C = U // B
    tokens, heads = queries.shape[0], head_map.shape[0]
    kv_heads = keys.shape[1] // DH
    lh = heads // U
    pieces = plan.shape[1]
    stretch = tokens * U
    block = stretch // pieces
    assert B * C == U and C % kv_heads == 0 and tokens % block == 0
    geo = dict(
        B=B, U=U, C=C, lh=lh, kv_heads=kv_heads, block=block, pieces=pieces, tokens=tokens
    )
    bf16 = jnp.bfloat16
    group_shape = jax.ShapeDtypeStruct((lh, tokens, DH), bf16)
    piece_shape = jax.ShapeDtypeStruct((2, tokens, DH), bf16)
    sort_scratch = [pltpu.SMEM((heads,), jnp.int32)]
    axes = ("blk", "uly")
    y, z = lax.axis_index("blk"), lax.axis_index("uly")

    def permute(x, target, wanted=lambda y, z: True):
        pairs = [
            (a * U + b, target(a, b)[0] * U + target(a, b)[1])
            for a in range(B)
            for b in range(U)
            if wanted(a, b)
        ]
        return lax.ppermute(x, axes, pairs)

    def limit(mib):
        return pltpu.CompilerParams(vmem_limit_bytes=mib * 1024 * 1024)

    def call(kernel, out_shape, in_specs, args, mib, out_specs=VMEM, scratch=()):
        return pl.pallas_call(
            functools.partial(kernel, geo),
            out_shape=out_shape,
            in_specs=in_specs,
            out_specs=[out_specs] * len(out_shape) if isinstance(out_shape, list) else out_specs,
            scratch_shapes=scratch,
            compiler_params=limit(mib),
        )(*args)

    def in_hbm(x):
        return pltpu.with_memory_space_constraint(x, pltpu.HBM)

    def sent_on(x, target, wanted=lambda y, z: True):
        return permute(x, target, wanted)

    def beside(b, j, d):
        return (b // C + j) % B * C + (b + d) % C

    steps = [(m, d) for m in range(B) for d in range(C)]
    heads_row, lengths = head_map[None, :], doc_lengths[None, :]

    def table_shape(x):
        return jax.ShapeDtypeStruct(x.shape, x.dtype)

    packed = call(
        pack_kernel,
        [group_shape] * (B * C) + [piece_shape] * C + [table_shape(x) for x in (heads_row, lengths)],
        [HBM] * 5,
        tuple(in_hbm(x) for x in (heads_row, queries, keys, values, lengths)),
        6,
        scratch=[
            pltpu.SMEM((1, heads), jnp.int32),
            pltpu.VMEM((tokens, heads * DH), bf16),
            *sort_scratch,
            pltpu.SemaphoreType.DMA((4 + 2 * C,)),
        ],
    )
    groups, kv_parts = dict(zip(steps, packed)), packed[B * C : B * C + C]
    heads_row, lengths = packed[B * C + C :]
    own = [groups[0, d] for d in range(C)]
    kv_in = [
        sent_on(kv_parts[d], lambda a, b, j=j, d=d: (a, beside(b, j, d)))
        if j or d
        else kv_parts[0]
        for j in range(B)
        for d in range(C)
    ]
    crossed = [
        sent_on(groups[m, d], lambda a, b, m=m: ((a + m) % B, b))
        for m in range(1, B)
        for d in range(C)
    ]
    kv_own = call(
        gather_kv_kernel, jax.ShapeDtypeStruct((2, U, tokens, DH), bf16), [VMEM] * U, kv_in, 8
    )
    across = []
    for j in range(B):
        for d in range(C):
            x = own[d]
            for m in range(1, B):
                x = jnp.where((z // C + j + m - y) % B == 0, crossed[(m - 1) * C + d], x)
            if j or d:
                x = sent_on(x, lambda a, b, j=j, d=d: (a, beside(b, j, d)))
            across.append(x)
    kv_all = [kv_own] + [
        sent_on(
            kv_own, lambda a, b, m=m: ((a + m) % B, b), lambda a, b: B == 2 or b // C in (a, a + 1)
        )
        for m in range(1, B)
    ]
    early, late = arrivals(B, C)
    tiles = [(j, d) for j in range(B) for d in range(C)]
    kv_cat, done = call(
        lambda geo, *refs: attend_early_kernel(geo, early, *refs),
        [
            jax.ShapeDtypeStruct((2, 2 * U, tokens, DH), bf16),
            jax.ShapeDtypeStruct((len(early), lh, tokens, DH), bf16),
        ],
        [VMEM] * (1 + B + len(early)),
        (lengths, *kv_all, *(across[tiles.index(step)] for step in early)),
        16,
    )
    steps = [(db, dc) for db in reversed(range(B)) for dc in reversed(range(C))]
    results = call(
        lambda geo, *refs: attend_late_kernel(geo, early, late, steps, *refs),
        [group_shape] * len(steps),
        [HBM] + [VMEM] * (3 + len(late)),
        (
            in_hbm(plan),
            lengths,
            kv_cat,
            done,
            *(across[tiles.index(step)] for step in late),
        ),
        16,
        scratch=[
            pltpu.SMEM(plan.shape, jnp.int32),
            pltpu.VMEM((U, lh, tokens, DH), bf16),
            pltpu.SemaphoreType.DMA((1,)),
        ],
    )
    arrived = {}
    for (db, dc), x in zip(steps, results):
        if db or dc:
            x = sent_on(x, lambda a, b, db=db, dc=dc: ((a + db) % B, beside(b, 0, dc)))
        arrived[db, dc] = x
    return call(
        unpack_kernel,
        jax.ShapeDtypeStruct((tokens, heads * DH), bf16),
        [VMEM] * (1 + B * C),
        (heads_row, *(arrived[db, dc] for db in range(B) for dc in range(C))),
        4,
        out_specs=HBM,
        scratch=[*sort_scratch, pltpu.SemaphoreType.DMA((heads,))],
    )


def arrivals(B, C):
    tiles = [(j, d) for j in range(B) for d in range(C)]
    late = [step for step in tiles if step[0] and step[1]]
    return [step for step in tiles if step not in late], late


def solution(mesh):
    return jax.shard_map(
        body,
        mesh=mesh,
        in_specs=(
            P(("blk", "uly"), "tp"),
            P(("blk", "uly"), "tp"),
            P(("blk", "uly"), "tp"),
            P("tp"),
            P(),
            P(),
        ),
        out_specs=P(("blk", "uly"), "tp"),
        check_vma=False,
    )
```

```python
import functools
import math

import jax
import jax.numpy as jnp
from jax import lax
from jax.experimental import pallas as pl
from jax.experimental.pallas import tpu as pltpu
from jax.sharding import PartitionSpec as P


DH = 128
LOG2E = 1.4426950408889634


VMEM = pl.BlockSpec(memory_space=pltpu.VMEM)
HBM = pl.BlockSpec(memory_space=pltpu.HBM)


def sort_heads(map_ref, order_ref, kv_heads):
    heads = map_ref.shape[1]
    per = heads // kv_heads
    place = [kv * per for kv in range(kv_heads)]
    for h in range(heads):
        kv = map_ref[0, h]
        at = place[0]
        for n in range(1, kv_heads):
            at = jnp.where(kv == n, place[n], at)
        order_ref[at] = h
        place = [p + (kv == n).astype(jnp.int32) for n, p in enumerate(place)]


def pack_kernel(geo, map_hbm, q_hbm, k_hbm, v_hbm, lengths_hbm, *rest):
    B, C, lh, kv_heads = geo["B"], geo["C"], geo["lh"], geo["kv_heads"]
    outs, (map_ref, q_ref, order_ref, sem) = rest[:-4], rest[-4:]
    half = geo["tokens"] // 2
    y, z = lax.axis_index("blk"), lax.axis_index("uly")
    copies = [
        pltpu.make_async_copy(map_hbm, map_ref, sem.at[0]),
        pltpu.make_async_copy(q_hbm.at[:half], q_ref.at[:half], sem.at[1]),
        pltpu.make_async_copy(map_hbm, outs[-2], sem.at[2]),
        pltpu.make_async_copy(lengths_hbm, outs[-1], sem.at[3]),
    ]
    for d in range(C):
        col = pl.multiple_of(lax.rem(z + d, C) * kv_heads // C * DH, DH)
        for n, ref in enumerate((k_hbm, v_hbm)):
            copies.append(
                pltpu.make_async_copy(
                    ref.at[:, pl.ds(col, DH)], outs[B * C + d].at[n], sem.at[4 + d * 2 + n]
                )
            )
    second = pltpu.make_async_copy(q_hbm.at[half:], q_ref.at[half:], sem.at[4 + 2 * C])
    for copy in (*copies[:2], second, *copies[2:]):
        copy.start()
    copies[0].wait()
    sort_heads(map_ref, order_ref, kv_heads)
    for arrived, rows in ((copies[1], slice(0, half)), (second, slice(half, 2 * half))):
        arrived.wait()
        for m in range(B):
            for d in range(C):
                group = lax.rem(z + d, C) * B + lax.rem(y + m, B)
                for i in range(lh):
                    h = order_ref[group * lh + i]
                    outs[m * C + d][i, rows] = q_ref[rows, pl.ds(pl.multiple_of(h * DH, DH), DH)]
    for copy in copies[2:]:
        copy.wait()


def gather_kv_kernel(geo, *refs):
    B, C = geo["B"], geo["C"]
    z = lax.axis_index("uly")
    out = refs[-1]
    for j in range(B):
        for d in range(C):
            source = lax.rem(z // C - j + B, B) * C + lax.rem(lax.rem(z, C) - d + C, C)
            out[0, source] = refs[j * C + d][0]
            out[1, source] = refs[j * C + d][1]


def document_ends(lengths_ref):
    ends = []
    total = 0
    for n in range(lengths_ref.shape[1]):
        total = total + lengths_ref[0, n]
        ends.append(total)
    return ends


def attend_tile(geo, ends, kv_cat, q_ref, out_ref, at_out, tile):
    C, U, lh, tokens = geo["C"], geo["U"], geo["lh"], geo["tokens"]
    stretch = tokens * U
    s = lax.axis_index("uly") // C
    factor = LOG2E / math.sqrt(DH)
    grain = -(-(U + 1) // 5)
    widths = [*range(grain, U + 1, grain), U + 1]
    row = lax.broadcasted_iota(jnp.int32, (tokens, 1), 0)
    first = s * stretch + tile * tokens
    begin = 0
    for end in ends:
        begin = jnp.where(first >= end, end, begin)
    needed = s * U + tile - begin // tokens + 1
    at = row + first
    start = jnp.zeros((tokens, 1), jnp.int32)
    for end in ends:
        start = jnp.where(at >= end, end, start)

    def with_keys(width):
        low = tile + U + 1 - width
        span = width * tokens
        q = q_ref[...].reshape(lh * tokens, DH)
        k = kv_cat[0, pl.ds(low, width)].reshape(span, DH)
        v = kv_cat[1, pl.ds(low, width)].reshape(span, DH)
        score = lax.dot_general(
            q, k, (((1,), (1,)), ((), ())), preferred_element_type=jnp.float32
        )
        base = (s - 1) * stretch + low * tokens
        key = lax.broadcasted_iota(jnp.int32, (tokens, span), 1)
        seen = (key >= start - base) & (key <= at - base)
        score = jnp.where(seen[None], score.reshape(lh, tokens, span), -jnp.inf)
        top = jnp.max(score, axis=-1, keepdims=True)
        expo = jnp.exp2((score - top) * factor)
        norm = jnp.sum(expo, axis=-1, keepdims=True)
        summed = jnp.dot(
            expo.astype(jnp.bfloat16).reshape(lh * tokens, span),
            v,
            preferred_element_type=jnp.float32,
        )
        out_ref[at_out] = (summed.reshape(lh, tokens, DH) / norm).astype(jnp.bfloat16)

    less = 0
    for width in widths:
        fits = needed > less
        if width < U + 1:
            fits = fits & (needed <= width)
        pl.when(fits)(functools.partial(with_keys, width))
        less = width


def tile_of(geo, step):
    B, C = geo["B"], geo["C"]
    z = lax.axis_index("uly")
    return lax.rem(z // C - step[0] + B, B) * C + lax.rem(lax.rem(z, C) - step[1] + C, C)


def attend_early_kernel(geo, early, lengths_ref, *refs):
    B, C, U, tokens = geo["B"], geo["C"], geo["U"], geo["tokens"]
    kv_refs, refs = refs[:B], refs[B:]
    rows, (kv_cat, done) = refs[:-2], refs[-2:]
    y, s = lax.axis_index("blk"), lax.axis_index("uly") // C

    @pl.when(s == 0)
    def _():
        kv_cat[:, :U] = jnp.zeros((2, U, tokens, DH), kv_cat.dtype)

    for m in range(B):
        holder = lax.rem(y - m + B, B)

        @pl.when(holder == s)
        def _():
            kv_cat[:, U:] = kv_refs[m][...]

        @pl.when(holder == s - 1)
        def _():
            kv_cat[:, :U] = kv_refs[m][...]

    ends = document_ends(lengths_ref)
    for n, step in enumerate(early):
        attend_tile(geo, ends, kv_cat, rows[n], done, n, tile_of(geo, step))


def attend_late_kernel(geo, early, late, steps, plan_hbm, lengths_ref, kv_cat, done, *refs):
    B, C = geo["B"], geo["C"]
    block, pieces, tokens = geo["block"], geo["pieces"], geo["tokens"]
    rows, refs = refs[: len(late)], refs[len(late) :]
    outs, (plan_ref, all_done, sem) = refs[:-3], refs[-3:]
    y, z = lax.axis_index("blk"), lax.axis_index("uly")
    s, c = z // C, lax.rem(z, C)
    table = pltpu.make_async_copy(plan_hbm, plan_ref, sem.at[0])
    table.start()
    for n, step in enumerate(early):
        all_done[tile_of(geo, step)] = done[n]
    ends = document_ends(lengths_ref)
    for n, step in enumerate(late):
        tile = tile_of(geo, step)
        attend_tile(geo, ends, kv_cat, rows[n], all_done, tile, tile)
    table.wait()
    per_tile = tokens // block
    slots = pieces // (B * C)
    for out, (db, dc) in zip(outs, steps):
        slot = lax.rem(y + db, B) * (pieces // B) + lax.rem(c + dc, C) * slots
        for j in range(slots):
            p = plan_ref[s, slot + j]
            tile = p // per_tile
            inside = pl.multiple_of((p - tile * per_tile) * block, block)
            out[:, j * block : (j + 1) * block, :] = all_done[tile, :, pl.ds(inside, block), :]


def unpack_kernel(geo, map_ref, *rest):
    B, C, lh = geo["B"], geo["C"], geo["lh"]
    pieces, (out, order_ref, sem) = rest[:-3], rest[-3:]
    y, z = lax.axis_index("blk"), lax.axis_index("uly")
    sort_heads(map_ref, order_ref, geo["kv_heads"])
    copies = []
    for db in range(B):
        for dc in range(C):
            group = lax.rem(z - dc + C, C) * B + lax.rem(y - db + B, B)
            for i in range(lh):
                h = order_ref[group * lh + i]
                copy = pltpu.make_async_copy(
                    pieces[db * C + dc].at[i],
                    out.at[:, pl.ds(pl.multiple_of(h * DH, DH), DH)],
                    sem.at[(db * C + dc) * lh + i],
                )
                copy.start()
                copies.append(copy)
    for copy in copies:
        copy.wait()


def body(queries, keys, values, head_map, doc_lengths, plan):
    B, U = lax.axis_size("blk"), lax.axis_size("uly")
    C = U // B
    tokens, heads = queries.shape[0], head_map.shape[0]
    kv_heads = keys.shape[1] // DH
    lh = heads // U
    pieces = plan.shape[1]
    stretch = tokens * U
    block = stretch // pieces
    assert B * C == U and C % kv_heads == 0 and tokens % block == 0
    geo = dict(
        B=B, U=U, C=C, lh=lh, kv_heads=kv_heads, block=block, pieces=pieces, tokens=tokens
    )
    bf16 = jnp.bfloat16
    group_shape = jax.ShapeDtypeStruct((lh, tokens, DH), bf16)
    piece_shape = jax.ShapeDtypeStruct((2, tokens, DH), bf16)
    sort_scratch = [pltpu.SMEM((heads,), jnp.int32)]
    axes = ("blk", "uly")
    y, z = lax.axis_index("blk"), lax.axis_index("uly")

    def permute(x, target, wanted=lambda y, z: True):
        pairs = [
            (a * U + b, target(a, b)[0] * U + target(a, b)[1])
            for a in range(B)
            for b in range(U)
            if wanted(a, b)
        ]
        return lax.ppermute(x, axes, pairs)

    def limit(mib):
        return pltpu.CompilerParams(vmem_limit_bytes=mib * 1024 * 1024)

    def call(kernel, out_shape, in_specs, args, mib, out_specs=VMEM, scratch=()):
        return pl.pallas_call(
            functools.partial(kernel, geo),
            out_shape=out_shape,
            in_specs=in_specs,
            out_specs=[out_specs] * len(out_shape) if isinstance(out_shape, list) else out_specs,
            scratch_shapes=scratch,
            compiler_params=limit(mib),
        )(*args)

    def in_hbm(x):
        return pltpu.with_memory_space_constraint(x, pltpu.HBM)

    def sent_on(x, target, wanted=lambda y, z: True):
        return permute(x, target, wanted)

    def beside(b, j, d):
        return (b // C + j) % B * C + (b + d) % C

    steps = [(m, d) for m in range(B) for d in range(C)]
    heads_row, lengths = head_map[None, :], doc_lengths[None, :]

    def table_shape(x):
        return jax.ShapeDtypeStruct(x.shape, x.dtype)

    packed = call(
        pack_kernel,
        [group_shape] * (B * C) + [piece_shape] * C + [table_shape(x) for x in (heads_row, lengths)],
        [HBM] * 5,
        tuple(in_hbm(x) for x in (heads_row, queries, keys, values, lengths)),
        6,
        scratch=[
            pltpu.SMEM((1, heads), jnp.int32),
            pltpu.VMEM((tokens, heads * DH), bf16),
            *sort_scratch,
            pltpu.SemaphoreType.DMA((5 + 2 * C,)),
        ],
    )
    groups, kv_parts = dict(zip(steps, packed)), packed[B * C : B * C + C]
    heads_row, lengths = packed[B * C + C :]
    own = [groups[0, d] for d in range(C)]
    kv_in = [
        sent_on(kv_parts[d], lambda a, b, j=j, d=d: (a, beside(b, j, d)))
        if j or d
        else kv_parts[0]
        for j in range(B)
        for d in range(C)
    ]
    crossed = [
        sent_on(groups[m, d], lambda a, b, m=m: ((a + m) % B, b))
        for m in range(1, B)
        for d in range(C)
    ]
    kv_own = call(
        gather_kv_kernel, jax.ShapeDtypeStruct((2, U, tokens, DH), bf16), [VMEM] * U, kv_in, 8
    )
    across = []
    for j in range(B):
        for d in range(C):
            x = own[d]
            for m in range(1, B):
                x = jnp.where((z // C + j + m - y) % B == 0, crossed[(m - 1) * C + d], x)
            if j or d:
                x = sent_on(x, lambda a, b, j=j, d=d: (a, beside(b, j, d)))
            across.append(x)
    kv_all = [kv_own] + [
        sent_on(
            kv_own, lambda a, b, m=m: ((a + m) % B, b), lambda a, b: B == 2 or b // C in (a, a + 1)
        )
        for m in range(1, B)
    ]
    early, late = arrivals(B, C)
    tiles = [(j, d) for j in range(B) for d in range(C)]
    kv_cat, done = call(
        lambda geo, *refs: attend_early_kernel(geo, early, *refs),
        [
            jax.ShapeDtypeStruct((2, 2 * U, tokens, DH), bf16),
            jax.ShapeDtypeStruct((len(early), lh, tokens, DH), bf16),
        ],
        [VMEM] * (1 + B + len(early)),
        (lengths, *kv_all, *(across[tiles.index(step)] for step in early)),
        16,
    )
    steps = [(db, dc) for db in reversed(range(B)) for dc in reversed(range(C))]
    results = call(
        lambda geo, *refs: attend_late_kernel(geo, early, late, steps, *refs),
        [group_shape] * len(steps),
        [HBM] + [VMEM] * (3 + len(late)),
        (
            in_hbm(plan),
            lengths,
            kv_cat,
            done,
            *(across[tiles.index(step)] for step in late),
        ),
        16,
        scratch=[
            pltpu.SMEM(plan.shape, jnp.int32),
            pltpu.VMEM((U, lh, tokens, DH), bf16),
            pltpu.SemaphoreType.DMA((1,)),
        ],
    )
    arrived = {}
    for (db, dc), x in zip(steps, results):
        if db or dc:
            x = sent_on(x, lambda a, b, db=db, dc=dc: ((a + db) % B, beside(b, 0, dc)))
        arrived[db, dc] = x
    return call(
        unpack_kernel,
        jax.ShapeDtypeStruct((tokens, heads * DH), bf16),
        [VMEM] * (1 + B * C),
        (heads_row, *(arrived[db, dc] for db in range(B) for dc in range(C))),
        4,
        out_specs=HBM,
        scratch=[*sort_scratch, pltpu.SemaphoreType.DMA((heads,))],
    )


def arrivals(B, C):
    tiles = [(j, d) for j in range(B) for d in range(C)]
    late = [step for step in tiles if step[0] and step[1]]
    return [step for step in tiles if step not in late], late


def solution(mesh):
    return jax.shard_map(
        body,
        mesh=mesh,
        in_specs=(
            P(("blk", "uly"), "tp"),
            P(("blk", "uly"), "tp"),
            P(("blk", "uly"), "tp"),
            P("tp"),
            P(),
            P(),
        ),
        out_specs=P(("blk", "uly"), "tp"),
        check_vma=False,
    )
```
